256 devices in a mesh: seq: 128 (over x_lo, y, z, core), ch: 2 (over x_hi).
Axes of the slice: x: 4 (x_hi: 2, x_lo: 2; x = x_hi * 2 + x_lo), y: 4, z: 8, core: 2. Of those that a mesh axis runs over, the one named last changes fastest.
Arguments:
- query_input: bfloat16 [16384, 1024], P('seq', 'ch'), may hold values from -6 to 6
- key_input: bfloat16 [16384, 1024], P('seq', 'ch'), may hold values from -6 to 6
- value_input: bfloat16 [16384, 1024], P('seq', 'ch'), may hold values from -6 to 6
- short_kernel: float32 [3, 7, 1024], P(None, None, 'ch'), may hold values from -2 to 2
- residues: float32 [16, 1024], P(None, 'ch'), may hold values from -1.5 to 1.5
- rates: float32 [16, 1024], P(None, 'ch'), may hold values from 3.0517578e-05 to 0.03
- out_weight: bfloat16 [1024, 8192], P('ch'), may hold values from -0.1875 to 0.1875
Outputs:
- mixed: float32 [16384, 8192], P(('seq', 'ch'))
The draws below stay inside these ranges and needn't reach their ends.
All inputs are finite; a program needn't handle non-finite values.
Results may differ from the reference program's by a relative error of at most 0.015.
Values may be sent and summed in bfloat16 or wider, within the bound.
A program may use at most 64 MiB of HBM per device.

```python
import math
import jax
import jax.numpy as jnp
from jax import lax

D = 8192
C = 1024
KERNEL = 7
ORDER = 16
SEQ = 16384


def block_levels(stream_key, dims, split, low, top_value):
    loudness, own = 1.0, jax.random.fold_in(stream_key, 6)
    for axis_at, blocks in split:
        heights = jnp.exp(jax.random.uniform(jax.random.fold_in(own, axis_at), (blocks,), jnp.float32, low / len(split), top_value / len(split)))
        loudness = loudness * jnp.repeat(heights, dims[axis_at] // blocks).reshape([-1 if axis == axis_at else 1 for axis in range(len(dims))])
    return loudness


def noise(key, extent, deviation, most, split=(), kind=jnp.bfloat16):
    values = deviation * jax.random.normal(key, extent, jnp.float32)
    if split:
        values = values * block_levels(key, extent, split, -0.22, 0.18)
    return jnp.clip(values, -most, most).astype(kind)


def setup_inputs(seed: int = 0) -> dict:
    streams_of = jax.random.split(jax.random.key(seed), 8)
    query_input = noise(streams_of[0], (SEQ, C), 1.0, 6.0, ((0, 128), (1, 2)))
    key_input = noise(streams_of[1], (SEQ, C), 1.0, 6.0, ((0, 128), (1, 2)))
    value_input = noise(streams_of[2], (SEQ, C), 1.0, 6.0, ((0, 128), (1, 2)))
    short_kernel = noise(streams_of[3], (3, KERNEL, C), KERNEL ** -0.5, 2.0, ((2, 2),), jnp.float32)
    residues = noise(streams_of[4], (ORDER, C), 0.25, 1.5, ((1, 2),), jnp.float32)
    rates = jnp.clip(jnp.exp(math.log(0.03) - 6.89065 * jax.random.uniform(streams_of[5], (ORDER, C), jnp.float32) ** block_levels(streams_of[5], (ORDER, C), ((1, 2),), -0.2, 0.2)), 3.0517578125e-05, 0.03)
    out_weight = noise(streams_of[6], (C, D), C ** -0.5, 0.1875, ((0, 2),))
    return dict(query_input=query_input, key_input=key_input, value_input=value_input, short_kernel=short_kernel, residues=residues, rates=rates, out_weight=out_weight)


def short_causal(inputs, weights):
    kernel_taps = weights.shape[0]
    length = inputs.shape[0]
    padded = jnp.pad(inputs.astype(jnp.float32), ((kernel_taps - 1, 0), (0, 0)))
    summed = jnp.zeros(inputs.shape, jnp.float32)
    for offset in range(kernel_taps):
        start_row = kernel_taps - 1 - offset
        summed = summed + weights[offset][None, :] * padded[start_row:start_row + length]
    return summed

def impulse_response(residues, rates, positions):
    scale = residues * jnp.sqrt(2.0 * rates)

    def add_mode(carry, operands):
        amplitude, decay = operands
        return (carry + amplitude[None, :] * jnp.exp(-decay[None, :] * positions[:, None]), None)
    start_value = jnp.zeros((positions.shape[0], residues.shape[1]), jnp.float32)
    summed, unused = lax.scan(add_mode, start_value, (scale, rates))
    return summed

def reference(query_input, key_input, value_input, short_kernel, residues, rates, out_weight):
    query = short_causal(query_input, short_kernel[0]).astype(jnp.bfloat16)
    gated_input = short_causal(key_input, short_kernel[1]) * short_causal(value_input, short_kernel[2])
    positions = jnp.arange(SEQ, dtype=jnp.float32)
    impulse = impulse_response(residues, rates, positions)
    block_width = math.gcd(C, 64)
    groups = C // block_width

    def convolve(operands):
        signal, response = operands
        spectrum = jnp.fft.rfft(signal, n=2 * SEQ, axis=1) * jnp.fft.rfft(response, n=2 * SEQ, axis=1)
        return jnp.fft.irfft(spectrum, n=2 * SEQ, axis=1)[:, :SEQ]
    signals = gated_input.T.reshape(groups, block_width, SEQ)
    responses = impulse.T.reshape(groups, block_width, SEQ)
    long_out = lax.map(convolve, (signals, responses)).reshape(C, SEQ).T
    gated = (query.astype(jnp.float32) * long_out).astype(jnp.bfloat16)
    row_count = math.gcd(SEQ, 4096)

    def project(row_block):
        return jnp.dot(row_block, out_weight, preferred_element_type=jnp.float32)
    mixed = lax.map(project, gated.reshape(SEQ // row_count, row_count, C))
    return mixed.reshape(SEQ, D)
```

```python
import functools
import math

import jax
import jax.numpy as jnp
from jax import lax
from jax.experimental import pallas as pl
from jax.experimental.pallas import tpu as pltpu
from jax.sharding import PartitionSpec as P

SEQ_FACTORS = (2, 4, 8, 2)
MESH = pl.DeviceIdType.MESH
BLOCK = 8
TAIL = 16


def scan_kernel(
    query_hbm,
    key_hbm,
    value_hbm,
    short_ref,
    residue_ref,
    rate_ref,
    gated_ref,
    raw,
    ext,
    tails,
    query_buf,
    driven,
    local_states,
    entry_states,
    state_rows,
    powers,
    response,
    taps,
    own_total,
    pair_total,
    ring_in,
    ring_total,
    plane_in,
    carry_half,
    carry_in,
    load_sem,
    tail_send,
    tail_recv,
    pair_send,
    pair_recv,
    ring_send,
    ring_recv,
    plane_send,
    plane_recv,
    half_send,
    half_recv,
):
    nx, ny, nz, nc = SEQ_FACTORS
    planes = nx * ny
    devices = planes * nz * nc
    tokens, width = query_buf.shape
    half = width // 2
    blocks = tokens // BLOCK
    me = lax.axis_index("seq")
    ch = lax.axis_index("ch")
    core = lax.rem(me, nc)
    chip = lax.div(me, nc)
    z = lax.rem(chip, nz)
    plane = lax.div(chip, nz)
    after = lax.rem(me + 1, devices)
    before = lax.rem(me + devices - 1, devices)
    sibling = chip * nc + (1 - core)

    loads = []
    for at, source in enumerate((key_hbm, value_hbm, query_hbm)):
        copy = pltpu.make_async_copy(source, raw.at[at], load_sem.at[at])
        copy.start()
        loads.append(copy)

    ring_peers = []
    for step in range(1, nz):
        ring_peers.append((plane * nz + lax.rem(z + step, nz)) * nc + core)
    plane_peers = []
    for step in range(1, planes):
        plane_peers.append((lax.rem(plane + step, planes) * nz + z) * nc + core)
    peers = [after, before, sibling] + ring_peers + plane_peers
    barrier = pltpu.get_barrier_semaphore()
    for peer in peers:
        pl.semaphore_signal(barrier, inc=1, device_id=(peer, ch), device_id_type=MESH)

    for part in range(2):
        columns = slice(part * half, (part + 1) * half)
        decay = jnp.exp(-rate_ref[:, columns])
        power = jnp.ones_like(decay)
        scaled = residue_ref[:, columns] * jnp.sqrt(2.0 * rate_ref[:, columns])
        for n in range(BLOCK):
            powers[n, part] = power
            tap = jnp.sum(scaled * power, axis=0, keepdims=True)
            rows = lax.broadcasted_iota(jnp.int32, (BLOCK, half), 0)
            taps[n, part] = jnp.where(rows >= n, jnp.broadcast_to(tap, (BLOCK, half)), 0.0)
            power = power * decay
        powers[BLOCK, part] = power
    ages = lax.broadcasted_iota(jnp.int32, (BLOCK, width), 0).astype(jnp.float32) + 1.0
    order = rate_ref.shape[0]
    for r in range(order):
        rate_row = rate_ref[r : r + 1, :]
        scale_row = residue_ref[r : r + 1, :] * jnp.sqrt(2.0 * rate_row)
        response[r] = scale_row * jnp.exp(-(ages * rate_row))

    pl.semaphore_wait(barrier, len(peers))
    for copy in loads:
        copy.wait()
    tail_copies = []
    for at, source in enumerate((key_hbm, value_hbm, query_hbm)):
        copy = pltpu.make_async_remote_copy(
            src_ref=source.at[pl.ds(tokens - TAIL, TAIL)],
            dst_ref=tails.at[at],
            send_sem=tail_send.at[at],
            recv_sem=tail_recv.at[at],
            device_id=(after, ch),
            device_id_type=MESH,
        )
        copy.start()
        tail_copies.append(copy)
    for copy in tail_copies:
        copy.wait_recv()
    for at in range(3):
        last = tails[at].astype(jnp.float32)[TAIL - BLOCK :]
        ext[at, 0:BLOCK] = jnp.where(me == 0, 0.0, last)
        ext[at, BLOCK:] = raw[at].astype(jnp.float32)

    def short_rows(at, filter_at, start):
        window = ext[at, pl.ds(start, 2 * BLOCK + BLOCK)]
        total = short_ref[filter_at, 0:1, :] * window[BLOCK:]
        for j in range(1, short_ref.shape[1]):
            total = total + short_ref[filter_at, j : j + 1, :] * window[BLOCK - j : 3 * BLOCK - j]
        return total

    @pl.loop(0, tokens // (2 * BLOCK))
    def _(i):
        start = pl.multiple_of(i * (2 * BLOCK), 2 * BLOCK)
        driven[pl.ds(start, 2 * BLOCK)] = short_rows(0, 1, start) * short_rows(1, 2, start)

    for part in range(2):
        columns = slice(part * half, (part + 1) * half)

        def advance(b, state):
            local_states[b, part] = state
            rows = driven[pl.ds(pl.multiple_of(b * BLOCK, BLOCK), BLOCK), columns]
            state = state * powers[BLOCK, part]
            for j in range(BLOCK):
                state = state + powers[BLOCK - 1 - j, part] * rows[j : j + 1, :]
            return state

        own_total[part] = lax.fori_loop(0, blocks, advance, jnp.zeros((order, half), jnp.float32))

    pair_copy = pltpu.make_async_remote_copy(
        src_ref=own_total,
        dst_ref=pair_total,
        send_sem=pair_send,
        recv_sem=pair_recv,
        device_id=(sibling, ch),
        device_id_type=MESH,
    )
    pair_copy.start()

    @pl.loop(0, tokens // (2 * BLOCK))
    def _(i):
        start = pl.multiple_of(i * (2 * BLOCK), 2 * BLOCK)
        query_buf[pl.ds(start, 2 * BLOCK)] = short_rows(2, 0, start).astype(query_buf.dtype)

    pair_copy.wait_recv()
    my_rates = jnp.where(core == 0, rate_ref[:, 0:half], rate_ref[:, half:])
    mine = own_total[core]
    theirs = pair_total[core]
    first = jnp.where(core == 0, mine, theirs)
    second = jnp.where(core == 0, theirs, mine)
    step_decay = jnp.exp(-(my_rates * float(tokens)))
    ring_in[z] = first * step_decay + second

    ring_copies = []
    for at, peer in enumerate(ring_peers):
        copy = pltpu.make_async_remote_copy(
            src_ref=ring_in.at[z],
            dst_ref=ring_in.at[z],
            send_sem=ring_send.at[at],
            recv_sem=ring_recv.at[at],
            device_id=(peer, ch),
            device_id_type=MESH,
        )
        copy.start()
        ring_copies.append(copy)
    for copy in ring_copies:
        copy.wait_recv()
    chip_decay = jnp.exp(-(my_rates * float(tokens * nc)))
    total = jnp.zeros((order, half), jnp.float32)
    before_me = total
    for at in range(nz):
        before_me = jnp.where(at == z, total, before_me)
        total = total * chip_decay + ring_in[at]
    plane_in[plane] = total

    plane_copies = []
    for at, peer in enumerate(plane_peers):
        copy = pltpu.make_async_remote_copy(
            src_ref=plane_in.at[plane],
            dst_ref=plane_in.at[plane],
            send_sem=plane_send.at[at],
            recv_sem=plane_recv.at[at],
            device_id=(peer, ch),
            device_id_type=MESH,
        )
        copy.start()
        plane_copies.append(copy)
    for copy in plane_copies:
        copy.wait_recv()
    row_decay = jnp.exp(-(my_rates * float(tokens * nc * nz)))
    total = jnp.zeros((order, half), jnp.float32)
    earlier = total
    for at in range(planes):
        earlier = jnp.where(at == plane, total, earlier)
        total = total * row_decay + plane_in[at]
    distance = (z * (tokens * nc)).astype(jnp.float32)
    carry_half[...] = before_me + earlier * jnp.exp(-(my_rates * distance))

    half_copy = pltpu.make_async_remote_copy(
        src_ref=carry_half,
        dst_ref=carry_in,
        send_sem=half_send,
        recv_sem=half_recv,
        device_id=(sibling, ch),
        device_id_type=MESH,
    )
    half_copy.start()
    half_copy.wait_recv()

    for part in range(2):
        columns = slice(part * half, (part + 1) * half)
        carry = jnp.where(core == part, carry_half[...], carry_in[...])
        decay = jnp.exp(-(rate_ref[:, columns] * float(tokens)))
        entry_states[part] = jnp.where(core == 0, carry, carry * decay + pair_total[part])

    @pl.loop(0, tokens // (2 * BLOCK))
    def _(i):
        start = pl.multiple_of(i * (2 * BLOCK), 2 * BLOCK)
        for part in range(2):
            columns = slice(part * half, (part + 1) * half)
            outs = []
            for sub in range(2):
                entry = entry_states[part]
                entry_states[part] = entry * powers[BLOCK, part]
                state = local_states[2 * i + sub, part] + entry
                rows = driven[pl.ds(pl.multiple_of(start + sub * BLOCK, BLOCK), BLOCK), columns]
                out = taps[0, part] * rows
                for n in range(1, BLOCK):
                    out = out + taps[n, part] * pltpu.roll(rows, n, 0)
                for r in range(order):
                    out = out + response[r, :, columns] * state[r : r + 1, :]
                outs.append(out)
            out = jnp.concatenate(outs, axis=0)
            query = query_buf[pl.ds(start, 2 * BLOCK), columns].astype(jnp.float32)
            gated_ref[pl.ds(start, 2 * BLOCK), columns] = (query * out).astype(gated_ref.dtype)

    for copy in tail_copies + ring_copies + plane_copies + [pair_copy, half_copy]:
        copy.wait_send()


def scan_call(query_input, key_input, value_input, short_kernel, residues, rates):
    nx, ny, nz, nc = SEQ_FACTORS
    tokens, width = query_input.shape
    order = rates.shape[0]
    half = width // 2
    f32 = jnp.float32
    dma = pltpu.SemaphoreType.DMA
    vmem = pl.BlockSpec(memory_space=pltpu.VMEM)
    anywhere = pl.BlockSpec(memory_space=pl.ANY)
    return pl.pallas_call(
        scan_kernel,
        out_shape=jax.ShapeDtypeStruct((tokens, width), jnp.bfloat16),
        in_specs=[anywhere] * 3 + [vmem] * 3,
        out_specs=vmem,
        scratch_shapes=[
            pltpu.VMEM((3, tokens, width), jnp.bfloat16),
            pltpu.VMEM((3, tokens + BLOCK, width), f32),
            pltpu.VMEM((3, TAIL, width), jnp.bfloat16),
            pltpu.VMEM((tokens, width), jnp.bfloat16),
            pltpu.VMEM((tokens, width), f32),
            pltpu.VMEM((tokens // BLOCK, 2, order, half), f32),
            pltpu.VMEM((2, order, half), f32),
            pltpu.VMEM((2, order, half), f32),
            pltpu.VMEM((BLOCK + 1, 2, order, half), f32),
            pltpu.VMEM((order, BLOCK, width), f32),
            pltpu.VMEM((BLOCK, 2, BLOCK, half), f32),
            pltpu.VMEM((2, order, half), f32),
            pltpu.VMEM((2, order, half), f32),
            pltpu.VMEM((nz, order, half), f32),
            pltpu.VMEM((order, half), f32),
            pltpu.VMEM((nx * ny, order, half), f32),
            pltpu.VMEM((order, half), f32),
            pltpu.VMEM((order, half), f32),
            dma((3,)),
            dma((3,)),
            dma((3,)),
            dma,
            dma,
            dma((nz - 1,)),
            dma((nz - 1,)),
            dma((nx * ny - 1,)),
            dma((nx * ny - 1,)),
            dma,
            dma,
        ],
        compiler_params=pltpu.CompilerParams(collective_id=0, has_side_effects=True),
        name="long_scan",
    )(query_input, key_input, value_input, short_kernel, residues, rates)


def per_device(query_input, key_input, value_input, short_kernel, residues, rates, out_weight):
    gated = scan_call(query_input, key_input, value_input, short_kernel, residues, rates)
    return lax.psum_scatter(
        jnp.dot(gated, out_weight, preferred_element_type=jnp.float32).astype(jnp.bfloat16),
        "ch",
        scatter_dimension=0,
        tiled=True,
    ).astype(jnp.float32)


def solution(mesh):
    assert math.prod(SEQ_FACTORS) == mesh.shape["seq"]
    return jax.shard_map(
        per_device,
        mesh=mesh,
        in_specs=(
            P("seq", "ch"),
            P("seq", "ch"),
            P("seq", "ch"),
            P(None, None, "ch"),
            P(None, "ch"),
            P(None, "ch"),
            P("ch", None),
        ),
        out_specs=P(("seq", "ch"), None),
        check_vma=False,
    )
```

```python
import functools
import math

import jax
import jax.numpy as jnp
from jax import lax
from jax.experimental import pallas as pl
from jax.experimental.pallas import tpu as pltpu
from jax.sharding import PartitionSpec as P

SEQ_FACTORS = (2, 4, 8, 2)
MESH = pl.DeviceIdType.MESH
BLOCK = 8
TAIL = 16
COLOURS = 8
CHUNKS = ((0, 96), (96, 80), (176, 96), (272, 80), (352, 80), (432, 80))
PARTS = ((0, 176), (176, 176), (352, 160))
DIRECTIONS = ("x", "y+", "y-", "z+", "z-")
SECOND = {
    "x": (-1, 2, "z+"),
    "y+": (-1, 1, "z+"),
    "y-": (1, 1, "z-"),
    "z+": (-2, 0, "y+"),
    "z-": (2, 0, "y-"),
}


def scan_kernel(
    query_hbm,
    key_hbm,
    value_hbm,
    short_ref,
    residue_ref,
    rate_ref,
    weight_hbm,
    out_ref,
    own_weight,
    other_weight,
    gated_ref,
    rows_in,
    partial,
    to_sibling,
    raw,
    ext,
    tails,
    query_buf,
    driven,
    local_states,
    entry_states,
    state_rows,
    powers,
    response,
    taps,
    own_total,
    pair_total,
    ring_in,
    ring_total,
    plane_in,
    carry_half,
    carry_in,
    load_sem,
    tail_send,
    tail_recv,
    pair_send,
    pair_recv,
    ring_send,
    ring_recv,
    plane_send,
    plane_recv,
    half_send,
    half_recv,
    weight_sem,
    cross_send,
    cross_recv,
    spread_send,
    spread_recv,
    second_send,
    second_recv,
    rows_send,
    rows_recv,
    result_send,
    result_recv,
):
    nx, ny, nz, nc = SEQ_FACTORS
    planes = nx * ny
    devices = planes * nz * nc
    tokens, width = query_buf.shape
    half = width // 2
    blocks = tokens // BLOCK
    me = lax.axis_index("seq")
    ch = lax.axis_index("ch")
    core = lax.rem(me, nc)
    chip = lax.div(me, nc)
    z = lax.rem(chip, nz)
    plane = lax.div(chip, nz)
    after = lax.rem(me + 1, devices)
    before = lax.rem(me + devices - 1, devices)
    sibling = chip * nc + (1 - core)

    loads = []
    for at, source in enumerate((key_hbm, value_hbm, query_hbm)):
        copy = pltpu.make_async_copy(source, raw.at[at], load_sem.at[at])
        copy.start()
        loads.append(copy)

    ring_peers = []
    for step in range(1, nz):
        ring_peers.append((plane * nz + lax.rem(z + step, nz)) * nc + core)
    plane_peers = []
    for step in range(1, planes):
        plane_peers.append((lax.rem(plane + step, planes) * nz + z) * nc + core)
    x_low = lax.div(plane, ny)
    y = lax.rem(plane, ny)
    other = 1 - ch

    def seq_at(x_at, y_at, z_at):
        return ((x_at * ny + y_at) * nz + z_at) * nc + core

    neighbours = {
        "x": seq_at(1 - x_low, y, z),
        "y+": seq_at(x_low, lax.rem(y + 1, ny), z),
        "y-": seq_at(x_low, lax.rem(y + ny - 1, ny), z),
        "z+": seq_at(x_low, y, lax.rem(z + 1, nz)),
        "z-": seq_at(x_low, y, lax.rem(z + nz - 1, nz)),
    }
    across = neighbours["x"]
    peers = [(peer, ch) for peer in [after, before, sibling] + ring_peers + plane_peers]
    peers += [(across, other), (me, other), (sibling, other)]
    barrier = pltpu.get_barrier_semaphore()
    for peer in peers:
        pl.semaphore_signal(barrier, inc=1, device_id=peer, device_id_type=MESH)

    depth, own_columns = own_weight.shape
    piece_columns = own_columns // COLOURS
    first_column = core * own_columns
    colour = lax.rem(4 * x_low + 2 * y + z, COLOURS)

    def shifted(by):
        return lax.rem(colour + by + COLOURS, COLOURS)

    weight_copy = pltpu.make_async_copy(
        weight_hbm.at[:, pl.ds(pl.multiple_of(first_column, own_columns), own_columns)],
        own_weight,
        weight_sem,
    )

    def cross_copy(at, piece, start, size):
        column = pl.multiple_of(first_column + piece * piece_columns, piece_columns)
        return pltpu.make_async_remote_copy(
            src_ref=weight_hbm.at[pl.ds(start, size), pl.ds(column, piece_columns)],
            dst_ref=other_weight.at[piece, pl.ds(start, size)],
            send_sem=cross_send.at[at],
            recv_sem=cross_recv.at[at],
            device_id=(across, other),
            device_id_type=MESH,
        )

    cross_copies = [
        cross_copy(at, shifted(4), start, size) for at, (start, size) in enumerate(CHUNKS)
    ]
    cross_copies.append(cross_copy(len(CHUNKS), shifted(1), *PARTS[2]))

    def passed_on(direction, piece, start, size, send_sem, recv_sem):
        return pltpu.make_async_remote_copy(
            src_ref=other_weight.at[piece, pl.ds(start, size)],
            dst_ref=other_weight.at[piece, pl.ds(start, size)],
            send_sem=send_sem,
            recv_sem=recv_sem,
            device_id=(neighbours[direction], ch),
            device_id_type=MESH,
        )

    spread_copies = {}
    second_copies = {}
    for to, direction in enumerate(DIRECTIONS):
        for at, (start, size) in enumerate(CHUNKS):
            spread_copies[direction, at] = passed_on(
                direction, colour, start, size, spread_send.at[to, at], spread_recv.at[to, at]
            )
        by, part, _ = SECOND[direction]
        second_copies[direction] = passed_on(
            direction, shifted(by), *PARTS[part], second_send.at[to], second_recv.at[to]
        )

    def spread(at):
        cross_copies[at].wait_recv()
        for direction in DIRECTIONS:
            spread_copies[direction, at].start()

    def second_hop(part):
        for direction in DIRECTIONS:
            by, its_part, came = SECOND[direction]
            if its_part == part:
                for at in (2 * part, 2 * part + 1):
                    if (came, at) not in arrived:
                        arrived.add((came, at))
                        spread_copies[came, at].wait_recv()
                second_copies[direction].start()

    arrived = set()

    for part in range(2):
        columns = slice(part * half, (part + 1) * half)
        decay = jnp.exp(-rate_ref[:, columns])
        power = jnp.ones_like(decay)
        scaled = residue_ref[:, columns] * jnp.sqrt(2.0 * rate_ref[:, columns])
        for n in range(BLOCK):
            powers[n, part] = power
            tap = jnp.sum(scaled * power, axis=0, keepdims=True)
            rows = lax.broadcasted_iota(jnp.int32, (BLOCK, half), 0)
            taps[n, part] = jnp.where(rows >= n, jnp.broadcast_to(tap, (BLOCK, half)), 0.0)
            power = power * decay
        powers[BLOCK, part] = power
    ages = lax.broadcasted_iota(jnp.int32, (BLOCK, width), 0).astype(jnp.float32) + 1.0
    order = rate_ref.shape[0]
    for r in range(order):
        rate_row = rate_ref[r : r + 1, :]
        scale_row = residue_ref[r : r + 1, :] * jnp.sqrt(2.0 * rate_row)
        response[r] = scale_row * jnp.exp(-(ages * rate_row))

    pl.semaphore_wait(barrier, len(peers))
    for copy in loads:
        copy.wait()
    tail_copies = []
    for at, source in enumerate((key_hbm, value_hbm, query_hbm)):
        copy = pltpu.make_async_remote_copy(
            src_ref=source.at[pl.ds(tokens - TAIL, TAIL)],
            dst_ref=tails.at[at],
            send_sem=tail_send.at[at],
            recv_sem=tail_recv.at[at],
            device_id=(after, ch),
            device_id_type=MESH,
        )
        copy.start()
        tail_copies.append(copy)
    for copy in cross_copies:
        copy.start()
    weight_copy.start()
    for copy in tail_copies:
        copy.wait_recv()
    for at in range(3):
        last = tails[at].astype(jnp.float32)[TAIL - BLOCK :]
        ext[at, 0:BLOCK] = jnp.where(me == 0, 0.0, last)
        ext[at, BLOCK:] = raw[at].astype(jnp.float32)

    def short_rows(at, filter_at, start):
        window = ext[at, pl.ds(start, 2 * BLOCK + BLOCK)]
        total = short_ref[filter_at, 0:1, :] * window[BLOCK:]
        for j in range(1, short_ref.shape[1]):
            total = total + short_ref[filter_at, j : j + 1, :] * window[BLOCK - j : 3 * BLOCK - j]
        return total

    @pl.loop(0, tokens // (2 * BLOCK))
    def _(i):
        start = pl.multiple_of(i * (2 * BLOCK), 2 * BLOCK)
        driven[pl.ds(start, 2 * BLOCK)] = short_rows(0, 1, start) * short_rows(1, 2, start)

    for part in range(2):
        columns = slice(part * half, (part + 1) * half)

        def advance(b, state):
            local_states[b, part] = state
            rows = driven[pl.ds(pl.multiple_of(b * BLOCK, BLOCK), BLOCK), columns]
            state = state * powers[BLOCK, part]
            for j in range(BLOCK):
                state = state + powers[BLOCK - 1 - j, part] * rows[j : j + 1, :]
            return state

        own_total[part] = lax.fori_loop(0, blocks, advance, jnp.zeros((order, half), jnp.float32))

    pair_copy = pltpu.make_async_remote_copy(
        src_ref=own_total,
        dst_ref=pair_total,
        send_sem=pair_send,
        recv_sem=pair_recv,
        device_id=(sibling, ch),
        device_id_type=MESH,
    )
    pair_copy.start()

    @pl.loop(0, tokens // (2 * BLOCK))
    def _(i):
        start = pl.multiple_of(i * (2 * BLOCK), 2 * BLOCK)
        query_buf[pl.ds(start, 2 * BLOCK)] = short_rows(2, 0, start).astype(query_buf.dtype)

    spread(0)
    pair_copy.wait_recv()
    my_rates = jnp.where(core == 0, rate_ref[:, 0:half], rate_ref[:, half:])
    mine = own_total[core]
    theirs = pair_total[core]
    first = jnp.where(core == 0, mine, theirs)
    second = jnp.where(core == 0, theirs, mine)
    step_decay = jnp.exp(-(my_rates * float(tokens)))
    ring_in[z] = first * step_decay + second

    ring_copies = []
    for at, peer in enumerate(ring_peers):
        copy = pltpu.make_async_remote_copy(
            src_ref=ring_in.at[z],
            dst_ref=ring_in.at[z],
            send_sem=ring_send.at[at],
            recv_sem=ring_recv.at[at],
            device_id=(peer, ch),
            device_id_type=MESH,
        )
        copy.start()
        ring_copies.append(copy)
    spread(1)
    spread(2)
    for copy in ring_copies:
        copy.wait_recv()
    chip_decay = jnp.exp(-(my_rates * float(tokens * nc)))
    total = jnp.zeros((order, half), jnp.float32)
    before_me = total
    for at in range(nz):
        before_me = jnp.where(at == z, total, before_me)
        total = total * chip_decay + ring_in[at]
    plane_in[plane] = total

    plane_copies = []
    for at, peer in enumerate(plane_peers):
        copy = pltpu.make_async_remote_copy(
            src_ref=plane_in.at[plane],
            dst_ref=plane_in.at[plane],
            send_sem=plane_send.at[at],
            recv_sem=plane_recv.at[at],
            device_id=(peer, ch),
            device_id_type=MESH,
        )
        copy.start()
        plane_copies.append(copy)
    spread(3)
    spread(4)
    for copy in plane_copies:
        copy.wait_recv()
    row_decay = jnp.exp(-(my_rates * float(tokens * nc * nz)))
    total = jnp.zeros((order, half), jnp.float32)
    earlier = total
    for at in range(planes):
        earlier = jnp.where(at == plane, total, earlier)
        total = total * row_decay + plane_in[at]
    distance = (z * (tokens * nc)).astype(jnp.float32)
    carry_half[...] = before_me + earlier * jnp.exp(-(my_rates * distance))

    half_copy = pltpu.make_async_remote_copy(
        src_ref=carry_half,
        dst_ref=carry_in,
        send_sem=half_send,
        recv_sem=half_recv,
        device_id=(sibling, ch),
        device_id_type=MESH,
    )
    half_copy.start()
    spread(5)
    second_hop(0)
    half_copy.wait_recv()

    for part in range(2):
        columns = slice(part * half, (part + 1) * half)
        carry = jnp.where(core == part, carry_half[...], carry_in[...])
        decay = jnp.exp(-(rate_ref[:, columns] * float(tokens)))
        entry_states[part] = jnp.where(core == 0, carry, carry * decay + pair_total[part])

    @pl.loop(0, tokens // (2 * BLOCK))
    def _(i):
        start = pl.multiple_of(i * (2 * BLOCK), 2 * BLOCK)
        for part in range(2):
            columns = slice(part * half, (part + 1) * half)
            outs = []
            for sub in range(2):
                entry = entry_states[part]
                entry_states[part] = entry * powers[BLOCK, part]
                state = local_states[2 * i + sub, part] + entry
                rows = driven[pl.ds(pl.multiple_of(start + sub * BLOCK, BLOCK), BLOCK), columns]
                out = taps[0, part] * rows
                for n in range(1, BLOCK):
                    out = out + taps[n, part] * pltpu.roll(rows, n, 0)
                for r in range(order):
                    out = out + response[r, :, columns] * state[r : r + 1, :]
                outs.append(out)
            out = jnp.concatenate(outs, axis=0)
            query = query_buf[pl.ds(start, 2 * BLOCK), columns].astype(jnp.float32)
            gated_ref[pl.ds(start, 2 * BLOCK), columns] = (query * out).astype(gated_ref.dtype)

    out_rows = tokens // 2
    keep = pl.multiple_of(ch * out_rows, out_rows)
    give = pl.multiple_of(other * out_rows, out_rows)
    rows_copies = []
    for at, (source, slot, place, target) in enumerate(
        (
            (give, 1, 0, (me, other)),
            (give, 1, 1, (sibling, other)),
            (keep, 0, 1, (sibling, ch)),
        )
    ):
        copy = pltpu.make_async_remote_copy(
            src_ref=gated_ref.at[pl.ds(source, out_rows)],
            dst_ref=rows_in.at[slot, pl.ds(place * out_rows, out_rows)],
            send_sem=rows_send.at[at],
            recv_sem=rows_recv.at[at],
            device_id=target,
            device_id_type=MESH,
        )
        copy.start()
        rows_copies.append(copy)
    second_hop(1)
    second_hop(2)
    rows_in[0, 0:out_rows] = gated_ref[pl.ds(keep, out_rows)]
    weight_copy.wait()
    rows_copies[2].wait_recv()

    @pl.loop(0, COLOURS)
    def _(n):
        columns = pl.ds(pl.multiple_of(n * piece_columns, piece_columns), piece_columns)
        partial[n] = jnp.dot(rows_in[0], own_weight[:, columns], preferred_element_type=jnp.float32)

    for direction in DIRECTIONS:
        for at in range(len(CHUNKS)):
            if (direction, at) not in arrived:
                spread_copies[direction, at].wait_recv()
        second_copies[direction].wait_recv()
    cross_copies[-1].wait_recv()
    rows_copies[0].wait_recv()
    rows_copies[1].wait_recv()

    def result_copy(n):
        column = pl.multiple_of(first_column + n * piece_columns, piece_columns)
        return pltpu.make_async_remote_copy(
            src_ref=to_sibling.at[n],
            dst_ref=out_ref.at[:, pl.ds(column, piece_columns)],
            send_sem=result_send.at[n],
            recv_sem=result_recv.at[n],
            device_id=(sibling, ch),
            device_id_type=MESH,
        )

    @pl.loop(0, COLOURS)
    def _(n):
        column = pl.multiple_of(first_column + n * piece_columns, piece_columns)
        total = partial[n] + jnp.dot(
            rows_in[1], other_weight[n], preferred_element_type=jnp.float32
        )
        to_sibling[n] = total[out_rows:]
        result_copy(n).start()
        out_ref[:, pl.ds(column, piece_columns)] = total[:out_rows]

    @pl.loop(0, COLOURS)
    def _(n):
        result_copy(n).wait()

    for copy in tail_copies + ring_copies + plane_copies + [pair_copy, half_copy]:
        copy.wait_send()
    for copy in cross_copies + rows_copies:
        copy.wait_send()
    for copy in list(spread_copies.values()) + list(second_copies.values()):
        copy.wait_send()


def scan_call(query_input, key_input, value_input, short_kernel, residues, rates, out_weight):
    nx, ny, nz, nc = SEQ_FACTORS
    tokens, width = query_input.shape
    order = rates.shape[0]
    half = width // 2
    columns = out_weight.shape[1]
    out_rows = tokens // 2
    piece_columns = columns // nc // COLOURS
    f32 = jnp.float32
    bf16 = jnp.bfloat16
    dma = pltpu.SemaphoreType.DMA
    vmem = pl.BlockSpec(memory_space=pltpu.VMEM)
    anywhere = pl.BlockSpec(memory_space=pl.ANY)
    return pl.pallas_call(
        scan_kernel,
        out_shape=jax.ShapeDtypeStruct((out_rows, columns), f32),
        in_specs=[anywhere] * 3 + [vmem] * 3 + [anywhere],
        out_specs=vmem,
        scratch_shapes=[
            pltpu.VMEM((width, columns // nc), bf16),
            pltpu.VMEM((COLOURS, width, piece_columns), bf16),
            pltpu.VMEM((tokens, width), bf16),
            pltpu.VMEM((2, tokens, width), bf16),
            pltpu.VMEM((COLOURS, tokens, piece_columns), f32),
            pltpu.VMEM((COLOURS, out_rows, piece_columns), f32),
            pltpu.VMEM((3, tokens, width), jnp.bfloat16),
            pltpu.VMEM((3, tokens + BLOCK, width), f32),
            pltpu.VMEM((3, TAIL, width), jnp.bfloat16),
            pltpu.VMEM((tokens, width), jnp.bfloat16),
            pltpu.VMEM((tokens, width), f32),
            pltpu.VMEM((tokens // BLOCK, 2, order, half), f32),
            pltpu.VMEM((2, order, half), f32),
            pltpu.VMEM((2, order, half), f32),
            pltpu.VMEM((BLOCK + 1, 2, order, half), f32),
            pltpu.VMEM((order, BLOCK, width), f32),
            pltpu.VMEM((BLOCK, 2, BLOCK, half), f32),
            pltpu.VMEM((2, order, half), f32),
            pltpu.VMEM((2, order, half), f32),
            pltpu.VMEM((nz, order, half), f32),
            pltpu.VMEM((order, half), f32),
            pltpu.VMEM((nx * ny, order, half), f32),
            pltpu.VMEM((order, half), f32),
            pltpu.VMEM((order, half), f32),
            dma((3,)),
            dma((3,)),
            dma((3,)),
            dma,
            dma,
            dma((nz - 1,)),
            dma((nz - 1,)),
            dma((nx * ny - 1,)),
            dma((nx * ny - 1,)),
            dma,
            dma,
            dma,
            dma((len(CHUNKS) + 1,)),
            dma((len(CHUNKS) + 1,)),
            dma((len(DIRECTIONS), len(CHUNKS))),
            dma((len(DIRECTIONS), len(CHUNKS))),
            dma((len(DIRECTIONS),)),
            dma((len(DIRECTIONS),)),
            dma((3,)),
            dma((3,)),
            dma((COLOURS,)),
            dma((COLOURS,)),
        ],
        compiler_params=pltpu.CompilerParams(collective_id=0, has_side_effects=True),
        name="long_scan",
    )(query_input, key_input, value_input, short_kernel, residues, rates, out_weight)


def per_device(query_input, key_input, value_input, short_kernel, residues, rates, out_weight):
    return scan_call(
        query_input, key_input, value_input, short_kernel, residues, rates, out_weight
    )


def solution(mesh):
    assert math.prod(SEQ_FACTORS) == mesh.shape["seq"]
    return jax.shard_map(
        per_device,
        mesh=mesh,
        in_specs=(
            P("seq", "ch"),
            P("seq", "ch"),
            P("seq", "ch"),
            P(None, None, "ch"),
            P(None, "ch"),
            P(None, "ch"),
            P("ch", None),
        ),
        out_specs=P(("seq", "ch"), None),
        check_vma=False,
    )
```

```python
import functools
import math

import jax
import jax.numpy as jnp
from jax import lax
from jax.experimental import pallas as pl
from jax.experimental.pallas import tpu as pltpu
from jax.sharding import PartitionSpec as P

SEQ_FACTORS = (2, 4, 8, 2)
MESH = pl.DeviceIdType.MESH
BLOCK = 8
TAIL = 16
COLOURS = 8
CHUNKS = ((0, 96), (96, 80), (176, 96), (272, 80), (352, 80), (432, 80))
PARTS = ((0, 176), (176, 176), (352, 160))
DIRECTIONS = ("x", "y+", "y-", "z+", "z-")
SECOND = {
    "x": (-1, 2, "z+"),
    "y+": (-1, 1, "z+"),
    "y-": (1, 1, "z-"),
    "z+": (-2, 0, "y+"),
    "z-": (2, 0, "y-"),
}


def scan_kernel(
    query_hbm,
    key_hbm,
    value_hbm,
    short_ref,
    residue_ref,
    rate_ref,
    weight_hbm,
    out_ref,
    own_weight,
    other_weight,
    gated_ref,
    rows_in,
    partial,
    to_sibling,
    raw,
    ext,
    tails,
    query_buf,
    driven,
    local_states,
    entry_states,
    state_rows,
    powers,
    response,
    taps,
    own_total,
    pair_total,
    ring_in,
    ring_total,
    plane_in,
    carry_half,
    carry_in,
    load_sem,
    tail_send,
    tail_recv,
    pair_send,
    pair_recv,
    ring_send,
    ring_recv,
    plane_send,
    plane_recv,
    half_send,
    half_recv,
    weight_sem,
    cross_send,
    cross_recv,
    spread_send,
    spread_recv,
    second_send,
    second_recv,
    rows_send,
    rows_recv,
    result_send,
    result_recv,
):
    nx, ny, nz, nc = SEQ_FACTORS
    planes = nx * ny
    devices = planes * nz * nc
    tokens, width = query_buf.shape
    half = width // 2
    blocks = tokens // BLOCK
    me = lax.axis_index("seq")
    ch = lax.axis_index("ch")
    core = lax.rem(me, nc)
    chip = lax.div(me, nc)
    z = lax.rem(chip, nz)
    plane = lax.div(chip, nz)
    after = lax.rem(me + 1, devices)
    before = lax.rem(me + devices - 1, devices)
    sibling = chip * nc + (1 - core)

    loads = []
    for at, source in enumerate((key_hbm, value_hbm, query_hbm)):
        copy = pltpu.make_async_copy(source, raw.at[at], load_sem.at[at])
        copy.start()
        loads.append(copy)

    ring_peers = []
    for step in range(1, nz):
        ring_peers.append((plane * nz + lax.rem(z + step, nz)) * nc + core)
    plane_peers = []
    for step in range(1, planes):
        plane_peers.append((lax.rem(plane + step, planes) * nz + z) * nc + core)
    x_low = lax.div(plane, ny)
    y = lax.rem(plane, ny)
    other = 1 - ch

    def seq_at(x_at, y_at, z_at):
        return ((x_at * ny + y_at) * nz + z_at) * nc + core

    neighbours = {
        "x": seq_at(1 - x_low, y, z),
        "y+": seq_at(x_low, lax.rem(y + 1, ny), z),
        "y-": seq_at(x_low, lax.rem(y + ny - 1, ny), z),
        "z+": seq_at(x_low, y, lax.rem(z + 1, nz)),
        "z-": seq_at(x_low, y, lax.rem(z + nz - 1, nz)),
    }
    across = neighbours["x"]
    peers = [(peer, ch) for peer in [after, before, sibling] + ring_peers + plane_peers]
    peers += [(across, other), (me, other)]
    barrier = pltpu.get_barrier_semaphore()
    for peer in peers:
        pl.semaphore_signal(barrier, inc=1, device_id=peer, device_id_type=MESH)

    depth, own_columns = own_weight.shape
    piece_columns = own_columns // COLOURS
    first_column = core * own_columns
    colour = lax.rem(4 * x_low + 2 * y + z, COLOURS)

    def shifted(by):
        return lax.rem(colour + by + COLOURS, COLOURS)

    weight_copy = pltpu.make_async_copy(
        weight_hbm.at[:, pl.ds(pl.multiple_of(first_column, own_columns), own_columns)],
        own_weight,
        weight_sem,
    )

    def cross_copy(at, piece, start, size):
        column = pl.multiple_of(first_column + piece * piece_columns, piece_columns)
        return pltpu.make_async_remote_copy(
            src_ref=weight_hbm.at[pl.ds(start, size), pl.ds(column, piece_columns)],
            dst_ref=other_weight.at[piece, pl.ds(start, size)],
            send_sem=cross_send.at[at],
            recv_sem=cross_recv.at[at],
            device_id=(across, other),
            device_id_type=MESH,
        )

    cross_copies = [
        cross_copy(at, shifted(4), start, size) for at, (start, size) in enumerate(CHUNKS)
    ]
    cross_copies.append(cross_copy(len(CHUNKS), shifted(1), *PARTS[2]))

    def passed_on(direction, piece, start, size, send_sem, recv_sem):
        return pltpu.make_async_remote_copy(
            src_ref=other_weight.at[piece, pl.ds(start, size)],
            dst_ref=other_weight.at[piece, pl.ds(start, size)],
            send_sem=send_sem,
            recv_sem=recv_sem,
            device_id=(neighbours[direction], ch),
            device_id_type=MESH,
        )

    spread_copies = {}
    second_copies = {}
    for to, direction in enumerate(DIRECTIONS):
        for at, (start, size) in enumerate(CHUNKS):
            spread_copies[direction, at] = passed_on(
                direction, colour, start, size, spread_send.at[to, at], spread_recv.at[to, at]
            )
        by, part, _ = SECOND[direction]
        second_copies[direction] = passed_on(
            direction, shifted(by), *PARTS[part], second_send.at[to], second_recv.at[to]
        )

    def spread(at):
        cross_copies[at].wait_recv()
        if at + 2 < len(cross_copies):
            cross_copies[at + 2].start()
        for direction in DIRECTIONS:
            spread_copies[direction, at].start()

    def second_hop(part):
        for direction in DIRECTIONS:
            by, its_part, came = SECOND[direction]
            if its_part == part:
                for at in (2 * part, 2 * part + 1):
                    if (came, at) not in arrived:
                        arrived.add((came, at))
                        spread_copies[came, at].wait_recv()
                second_copies[direction].start()

    arrived = set()

    for part in range(2):
        columns = slice(part * half, (part + 1) * half)
        decay = jnp.exp(-rate_ref[:, columns])
        power = jnp.ones_like(decay)
        for n in range(BLOCK + 1):
            powers[n, part] = power
            power = power * decay
    order = rate_ref.shape[0]

    def output_tables():
        for part in range(2):
            columns = slice(part * half, (part + 1) * half)
            scaled = residue_ref[:, columns] * jnp.sqrt(2.0 * rate_ref[:, columns])
            rows = lax.broadcasted_iota(jnp.int32, (BLOCK, half), 0)
            for n in range(BLOCK):
                tap = jnp.sum(scaled * powers[n, part], axis=0, keepdims=True)
                taps[n, part] = jnp.where(rows >= n, jnp.broadcast_to(tap, (BLOCK, half)), 0.0)
        ages = lax.broadcasted_iota(jnp.int32, (BLOCK, width), 0).astype(jnp.float32) + 1.0
        for r in range(order):
            rate_row = rate_ref[r : r + 1, :]
            scale_row = residue_ref[r : r + 1, :] * jnp.sqrt(2.0 * rate_row)
            response[r] = scale_row * jnp.exp(-(ages * rate_row))

    pl.semaphore_wait(barrier, len(peers))
    for copy in loads:
        copy.wait()
    tail_copies = []
    for at, source in enumerate((key_hbm, value_hbm, query_hbm)):
        copy = pltpu.make_async_remote_copy(
            src_ref=source.at[pl.ds(tokens - TAIL, TAIL)],
            dst_ref=tails.at[at],
            send_sem=tail_send.at[at],
            recv_sem=tail_recv.at[at],
            device_id=(after, ch),
            device_id_type=MESH,
        )
        copy.start()
        tail_copies.append(copy)
    for copy in cross_copies[:2]:
        copy.start()
    weight_copy.start()
    for copy in tail_copies:
        copy.wait_recv()
    for at in range(3):
        last = tails[at].astype(jnp.float32)[TAIL - BLOCK :]
        ext[at, 0:BLOCK] = jnp.where(me == 0, 0.0, last)
        ext[at, BLOCK:] = raw[at].astype(jnp.float32)

    def short_rows(at, filter_at, start):
        window = ext[at, pl.ds(start, 2 * BLOCK + BLOCK)]
        total = short_ref[filter_at, 0:1, :] * window[BLOCK:]
        for j in range(1, short_ref.shape[1]):
            total = total + short_ref[filter_at, j : j + 1, :] * window[BLOCK - j : 3 * BLOCK - j]
        return total

    @pl.loop(0, tokens // (2 * BLOCK))
    def _(i):
        start = pl.multiple_of(i * (2 * BLOCK), 2 * BLOCK)
        driven[pl.ds(start, 2 * BLOCK)] = short_rows(0, 1, start) * short_rows(1, 2, start)

    for part in range(2):
        columns = slice(part * half, (part + 1) * half)

        def advance(b, state):
            local_states[b, part] = state
            rows = driven[pl.ds(pl.multiple_of(b * BLOCK, BLOCK), BLOCK), columns]
            state = state * powers[BLOCK, part]
            for j in range(BLOCK):
                state = state + powers[BLOCK - 1 - j, part] * rows[j : j + 1, :]
            return state

        own_total[part] = lax.fori_loop(0, blocks, advance, jnp.zeros((order, half), jnp.float32))

    pair_copy = pltpu.make_async_remote_copy(
        src_ref=own_total,
        dst_ref=pair_total,
        send_sem=pair_send,
        recv_sem=pair_recv,
        device_id=(sibling, ch),
        device_id_type=MESH,
    )
    pair_copy.start()

    @pl.loop(0, tokens // (2 * BLOCK))
    def _(i):
        start = pl.multiple_of(i * (2 * BLOCK), 2 * BLOCK)
        query_buf[pl.ds(start, 2 * BLOCK)] = short_rows(2, 0, start).astype(query_buf.dtype)

    spread(0)
    pair_copy.wait_recv()
    my_rates = jnp.where(core == 0, rate_ref[:, 0:half], rate_ref[:, half:])
    mine = own_total[core]
    theirs = pair_total[core]
    first = jnp.where(core == 0, mine, theirs)
    second = jnp.where(core == 0, theirs, mine)
    step_decay = jnp.exp(-(my_rates * float(tokens)))
    ring_in[z] = first * step_decay + second

    ring_copies = []
    for at, peer in enumerate(ring_peers):
        copy = pltpu.make_async_remote_copy(
            src_ref=ring_in.at[z],
            dst_ref=ring_in.at[z],
            send_sem=ring_send.at[at],
            recv_sem=ring_recv.at[at],
            device_id=(peer, ch),
            device_id_type=MESH,
        )
        copy.start()
        ring_copies.append(copy)
    output_tables()
    spread(1)
    spread(2)
    for copy in ring_copies:
        copy.wait_recv()
    chip_decay = jnp.exp(-(my_rates * float(tokens * nc)))
    total = jnp.zeros((order, half), jnp.float32)
    before_me = total
    for at in range(nz):
        before_me = jnp.where(at == z, total, before_me)
        total = total * chip_decay + ring_in[at]
    plane_in[plane] = total

    plane_copies = []
    for at, peer in enumerate(plane_peers):
        copy = pltpu.make_async_remote_copy(
            src_ref=plane_in.at[plane],
            dst_ref=plane_in.at[plane],
            send_sem=plane_send.at[at],
            recv_sem=plane_recv.at[at],
            device_id=(peer, ch),
            device_id_type=MESH,
        )
        copy.start()
        plane_copies.append(copy)
    spread(3)
    spread(4)
    second_hop(0)
    spread(5)
    for copy in plane_copies:
        copy.wait_recv()
    row_decay = jnp.exp(-(my_rates * float(tokens * nc * nz)))
    total = jnp.zeros((order, half), jnp.float32)
    earlier = total
    for at in range(planes):
        earlier = jnp.where(at == plane, total, earlier)
        total = total * row_decay + plane_in[at]
    distance = (z * (tokens * nc)).astype(jnp.float32)
    carry_half[...] = before_me + earlier * jnp.exp(-(my_rates * distance))

    half_copy = pltpu.make_async_remote_copy(
        src_ref=carry_half,
        dst_ref=carry_in,
        send_sem=half_send,
        recv_sem=half_recv,
        device_id=(sibling, ch),
        device_id_type=MESH,
    )
    half_copy.start()
    second_hop(1)
    half_copy.wait_recv()

    entries = []
    for part in range(2):
        columns = slice(part * half, (part + 1) * half)
        carry = jnp.where(core == part, carry_half[...], carry_in[...])
        decay = jnp.exp(-(rate_ref[:, columns] * float(tokens)))
        entries.append(jnp.where(core == 0, carry, carry * decay + pair_total[part]))
    out_rows = tokens // 2
    steps = out_rows // (2 * BLOCK)

    def output_half(which):
        for part in range(2):
            columns = slice(part * half, (part + 1) * half)
            decay = jnp.exp(-(rate_ref[:, columns] * float(out_rows)))
            entry_states[part] = jnp.where(which == 0, entries[part], entries[part] * decay)

        @pl.loop(0, steps)
        def _(step):
            i = which * steps + step
            start = pl.multiple_of(i * (2 * BLOCK), 2 * BLOCK)
            for part in range(2):
                columns = slice(part * half, (part + 1) * half)
                outs = []
                for sub in range(2):
                    entry = entry_states[part]
                    entry_states[part] = entry * powers[BLOCK, part]
                    state = local_states[2 * i + sub, part] + entry
                    rows = driven[pl.ds(pl.multiple_of(start + sub * BLOCK, BLOCK), BLOCK), columns]
                    out = taps[0, part] * rows
                    for n in range(1, BLOCK):
                        out = out + taps[n, part] * pltpu.roll(rows, n, 0)
                    for r in range(order):
                        out = out + response[r, :, columns] * state[r : r + 1, :]
                    outs.append(out)
                out = jnp.concatenate(outs, axis=0)
                query = query_buf[pl.ds(start, 2 * BLOCK), columns].astype(jnp.float32)
                gated_ref[pl.ds(start, 2 * BLOCK), columns] = (query * out).astype(gated_ref.dtype)

    keep = pl.multiple_of(ch * out_rows, out_rows)
    give = pl.multiple_of(other * out_rows, out_rows)
    arriving = rows_in.at[1, pl.ds(0, out_rows)]
    rows_copies = []
    for at, (source, slot, place, target) in enumerate(
        (
            (gated_ref.at[pl.ds(give, out_rows)], 1, 0, (me, other)),
            (gated_ref.at[pl.ds(keep, out_rows)], 0, 1, (sibling, ch)),
            (arriving, 1, 1, (sibling, ch)),
        )
    ):
        rows_copies.append(
            pltpu.make_async_remote_copy(
                src_ref=source,
                dst_ref=rows_in.at[slot, pl.ds(place * out_rows, out_rows)],
                send_sem=rows_send.at[at],
                recv_sem=rows_recv.at[at],
                device_id=target,
                device_id_type=MESH,
            )
        )
    output_half(other)
    rows_copies[0].start()
    second_hop(2)
    output_half(ch)
    rows_copies[1].start()
    rows_in[0, 0:out_rows] = gated_ref[pl.ds(keep, out_rows)]
    weight_copy.wait()
    rows_copies[1].wait_recv()

    @pl.loop(0, COLOURS)
    def _(n):
        columns = pl.ds(pl.multiple_of(n * piece_columns, piece_columns), piece_columns)
        partial[n] = jnp.dot(rows_in[0], own_weight[:, columns], preferred_element_type=jnp.float32)

    rows_copies[0].wait_recv()
    rows_copies[2].start()
    for direction in DIRECTIONS:
        for at in range(len(CHUNKS)):
            if (direction, at) not in arrived:
                spread_copies[direction, at].wait_recv()
        second_copies[direction].wait_recv()
    cross_copies[-1].wait_recv()
    rows_copies[2].wait_recv()

    def result_copy(n):
        column = pl.multiple_of(first_column + n * piece_columns, piece_columns)
        return pltpu.make_async_remote_copy(
            src_ref=to_sibling.at[n],
            dst_ref=out_ref.at[:, pl.ds(column, piece_columns)],
            send_sem=result_send.at[n],
            recv_sem=result_recv.at[n],
            device_id=(sibling, ch),
            device_id_type=MESH,
        )

    @pl.loop(0, COLOURS)
    def _(n):
        column = pl.multiple_of(first_column + n * piece_columns, piece_columns)
        total = partial[n] + jnp.dot(
            rows_in[1], other_weight[n], preferred_element_type=jnp.float32
        )
        total = total.astype(out_ref.dtype)
        to_sibling[n] = total[out_rows:]
        result_copy(n).start()
        out_ref[:, pl.ds(column, piece_columns)] = total[:out_rows]

    @pl.loop(0, COLOURS)
    def _(n):
        result_copy(n).wait()

    for copy in tail_copies + ring_copies + plane_copies + [pair_copy, half_copy]:
        copy.wait_send()
    for copy in cross_copies + rows_copies:
        copy.wait_send()
    for copy in list(spread_copies.values()) + list(second_copies.values()):
        copy.wait_send()


def scan_call(query_input, key_input, value_input, short_kernel, residues, rates, out_weight):
    nx, ny, nz, nc = SEQ_FACTORS
    tokens, width = query_input.shape
    order = rates.shape[0]
    half = width // 2
    columns = out_weight.shape[1]
    out_rows = tokens // 2
    piece_columns = columns // nc // COLOURS
    f32 = jnp.float32
    bf16 = jnp.bfloat16
    dma = pltpu.SemaphoreType.DMA
    vmem = pl.BlockSpec(memory_space=pltpu.VMEM)
    anywhere = pl.BlockSpec(memory_space=pl.ANY)
    return pl.pallas_call(
        scan_kernel,
        out_shape=jax.ShapeDtypeStruct((out_rows, columns), bf16),
        in_specs=[anywhere] * 3 + [vmem] * 3 + [anywhere],
        out_specs=vmem,
        scratch_shapes=[
            pltpu.VMEM((width, columns // nc), bf16),
            pltpu.VMEM((COLOURS, width, piece_columns), bf16),
            pltpu.VMEM((tokens, width), bf16),
            pltpu.VMEM((2, tokens, width), bf16),
            pltpu.VMEM((COLOURS, tokens, piece_columns), f32),
            pltpu.VMEM((COLOURS, out_rows, piece_columns), bf16),
            pltpu.VMEM((3, tokens, width), jnp.bfloat16),
            pltpu.VMEM((3, tokens + BLOCK, width), f32),
            pltpu.VMEM((3, TAIL, width), jnp.bfloat16),
            pltpu.VMEM((tokens, width), jnp.bfloat16),
            pltpu.VMEM((tokens, width), f32),
            pltpu.VMEM((tokens // BLOCK, 2, order, half), f32),
            pltpu.VMEM((2, order, half), f32),
            pltpu.VMEM((2, order, half), f32),
            pltpu.VMEM((BLOCK + 1, 2, order, half), f32),
            pltpu.VMEM((order, BLOCK, width), f32),
            pltpu.VMEM((BLOCK, 2, BLOCK, half), f32),
            pltpu.VMEM((2, order, half), f32),
            pltpu.VMEM((2, order, half), f32),
            pltpu.VMEM((nz, order, half), f32),
            pltpu.VMEM((order, half), f32),
            pltpu.VMEM((nx * ny, order, half), f32),
            pltpu.VMEM((order, half), f32),
            pltpu.VMEM((order, half), f32),
            dma((3,)),
            dma((3,)),
            dma((3,)),
            dma,
            dma,
            dma((nz - 1,)),
            dma((nz - 1,)),
            dma((nx * ny - 1,)),
            dma((nx * ny - 1,)),
            dma,
            dma,
            dma,
            dma((len(CHUNKS) + 1,)),
            dma((len(CHUNKS) + 1,)),
            dma((len(DIRECTIONS), len(CHUNKS))),
            dma((len(DIRECTIONS), len(CHUNKS))),
            dma((len(DIRECTIONS),)),
            dma((len(DIRECTIONS),)),
            dma((3,)),
            dma((3,)),
            dma((COLOURS,)),
            dma((COLOURS,)),
        ],
        compiler_params=pltpu.CompilerParams(collective_id=0, has_side_effects=True),
        name="long_scan",
    )(query_input, key_input, value_input, short_kernel, residues, rates, out_weight)


def per_device(query_input, key_input, value_input, short_kernel, residues, rates, out_weight):
    mixed = scan_call(
        query_input, key_input, value_input, short_kernel, residues, rates, out_weight
    )
    return mixed.astype(jnp.float32)


def solution(mesh):
    assert math.prod(SEQ_FACTORS) == mesh.shape["seq"]
    return jax.shard_map(
        per_device,
        mesh=mesh,
        in_specs=(
            P("seq", "ch"),
            P("seq", "ch"),
            P("seq", "ch"),
            P(None, None, "ch"),
            P(None, "ch"),
            P(None, "ch"),
            P("ch", None),
        ),
        out_specs=P(("seq", "ch"), None),
        check_vma=False,
    )
```

```python
import functools
import math

import jax
import jax.numpy as jnp
from jax import lax
from jax.experimental import pallas as pl
from jax.experimental.pallas import tpu as pltpu
from jax.sharding import PartitionSpec as P

SEQ_FACTORS = (2, 4, 8, 2)
MESH = pl.DeviceIdType.MESH
BLOCK = 8
TAIL = 16
COLOURS = 8
CHUNKS = ((0, 96), (96, 80), (176, 96), (272, 80), (352, 80), (432, 80))
PARTS = ((0, 176), (176, 176), (352, 160))
DIRECTIONS = ("x", "y+", "y-", "z+", "z-")
SECOND = {
    "x": (-1, 2, "z+"),
    "y+": (-1, 1, "z+"),
    "y-": (1, 1, "z-"),
    "z+": (-2, 0, "y+"),
    "z-": (2, 0, "y-"),
}


def scan_kernel(
    query_hbm,
    key_hbm,
    value_hbm,
    short_ref,
    residue_ref,
    rate_ref,
    weight_hbm,
    out_ref,
    own_weight,
    other_weight,
    gated_ref,
    rows_in,
    partial,
    to_sibling,
    raw,
    ext,
    tails,
    query_buf,
    driven,
    local_states,
    entry_states,
    state_rows,
    powers,
    response,
    taps,
    own_total,
    pair_total,
    ring_in,
    ring_total,
    plane_in,
    carry_half,
    carry_in,
    load_sem,
    tail_send,
    tail_recv,
    pair_send,
    pair_recv,
    ring_send,
    ring_recv,
    plane_send,
    plane_recv,
    half_send,
    half_recv,
    weight_sem,
    cross_send,
    cross_recv,
    spread_send,
    spread_recv,
    second_send,
    second_recv,
    rows_send,
    rows_recv,
    result_send,
    result_recv,
):
    nx, ny, nz, nc = SEQ_FACTORS
    planes = nx * ny
    devices = planes * nz * nc
    tokens, width = query_buf.shape
    half = width // 2
    blocks = tokens // BLOCK
    me = lax.axis_index("seq")
    ch = lax.axis_index("ch")
    core = lax.rem(me, nc)
    chip = lax.div(me, nc)
    z = lax.rem(chip, nz)
    plane = lax.div(chip, nz)
    after = lax.rem(me + 1, devices)
    before = lax.rem(me + devices - 1, devices)
    sibling = chip * nc + (1 - core)

    loads = []
    for at, source in enumerate((key_hbm, value_hbm, query_hbm)):
        copy = pltpu.make_async_copy(source, raw.at[at], load_sem.at[at])
        copy.start()
        loads.append(copy)

    ring_peers = []
    for step in range(1, nz):
        ring_peers.append((plane * nz + lax.rem(z + step, nz)) * nc + core)
    plane_peers = []
    for step in range(1, planes):
        plane_peers.append((lax.rem(plane + step, planes) * nz + z) * nc)
    x_low = lax.div(plane, ny)
    y = lax.rem(plane, ny)
    other = 1 - ch

    def seq_at(x_at, y_at, z_at):
        return ((x_at * ny + y_at) * nz + z_at) * nc + core

    neighbours = {
        "x": seq_at(1 - x_low, y, z),
        "y+": seq_at(x_low, lax.rem(y + 1, ny), z),
        "y-": seq_at(x_low, lax.rem(y + ny - 1, ny), z),
        "z+": seq_at(x_low, y, lax.rem(z + 1, nz)),
        "z-": seq_at(x_low, y, lax.rem(z + nz - 1, nz)),
    }
    across = neighbours["x"]
    peers = [(peer, ch) for peer in [after, before, sibling] + ring_peers]
    peers += [(peer + at, ch) for peer in plane_peers for at in range(nc)]
    peers += [(across, other), (me, other)]
    barrier = pltpu.get_barrier_semaphore()
    for peer in peers:
        pl.semaphore_signal(barrier, inc=1, device_id=peer, device_id_type=MESH)

    depth, own_columns = own_weight.shape
    piece_columns = own_columns // COLOURS
    first_column = core * own_columns
    colour = lax.rem(4 * x_low + 2 * y + z, COLOURS)

    def shifted(by):
        return lax.rem(colour + by + COLOURS, COLOURS)

    weight_copy = pltpu.make_async_copy(
        weight_hbm.at[:, pl.ds(pl.multiple_of(first_column, own_columns), own_columns)],
        own_weight,
        weight_sem,
    )

    def cross_copy(at, piece, start, size):
        column = pl.multiple_of(first_column + piece * piece_columns, piece_columns)
        return pltpu.make_async_remote_copy(
            src_ref=weight_hbm.at[pl.ds(start, size), pl.ds(column, piece_columns)],
            dst_ref=other_weight.at[piece, pl.ds(start, size)],
            send_sem=cross_send.at[at],
            recv_sem=cross_recv.at[at],
            device_id=(across, other),
            device_id_type=MESH,
        )

    cross_copies = [
        cross_copy(at, shifted(4), start, size) for at, (start, size) in enumerate(CHUNKS)
    ]
    cross_copies.append(cross_copy(len(CHUNKS), shifted(1), *PARTS[2]))

    def passed_on(direction, piece, start, size, send_sem, recv_sem):
        return pltpu.make_async_remote_copy(
            src_ref=other_weight.at[piece, pl.ds(start, size)],
            dst_ref=other_weight.at[piece, pl.ds(start, size)],
            send_sem=send_sem,
            recv_sem=recv_sem,
            device_id=(neighbours[direction], ch),
            device_id_type=MESH,
        )

    spread_copies = {}
    second_copies = {}
    for to, direction in enumerate(DIRECTIONS):
        for at, (start, size) in enumerate(CHUNKS):
            spread_copies[direction, at] = passed_on(
                direction, colour, start, size, spread_send.at[to, at], spread_recv.at[to, at]
            )
        by, part, _ = SECOND[direction]
        second_copies[direction] = passed_on(
            direction, shifted(by), *PARTS[part], second_send.at[to], second_recv.at[to]
        )

    def spread(at):
        cross_copies[at].wait_recv()
        if at + 2 < len(cross_copies):
            cross_copies[at + 2].start()
        for direction in DIRECTIONS:
            spread_copies[direction, at].start()

    def second_hop(part):
        for direction in DIRECTIONS:
            by, its_part, came = SECOND[direction]
            if its_part == part:
                for at in (2 * part, 2 * part + 1):
                    if (came, at) not in arrived:
                        arrived.add((came, at))
                        spread_copies[came, at].wait_recv()
                second_copies[direction].start()

    arrived = set()

    for part in range(2):
        columns = slice(part * half, (part + 1) * half)
        decay = jnp.exp(-rate_ref[:, columns])
        power = jnp.ones_like(decay)
        for n in range(BLOCK + 1):
            powers[n, part] = power
            power = power * decay
    order = rate_ref.shape[0]

    def output_tables():
        for part in range(2):
            columns = slice(part * half, (part + 1) * half)
            scaled = residue_ref[:, columns] * jnp.sqrt(2.0 * rate_ref[:, columns])
            rows = lax.broadcasted_iota(jnp.int32, (BLOCK, half), 0)
            for n in range(BLOCK):
                tap = jnp.sum(scaled * powers[n, part], axis=0, keepdims=True)
                taps[n, part] = jnp.where(rows >= n, jnp.broadcast_to(tap, (BLOCK, half)), 0.0)
        ages = lax.broadcasted_iota(jnp.int32, (BLOCK, width), 0).astype(jnp.float32) + 1.0
        for r in range(order):
            rate_row = rate_ref[r : r + 1, :]
            scale_row = residue_ref[r : r + 1, :] * jnp.sqrt(2.0 * rate_row)
            response[r] = scale_row * jnp.exp(-(ages * rate_row))

    pl.semaphore_wait(barrier, len(peers))
    for copy in loads:
        copy.wait()
    tail_copies = []
    for at, source in enumerate((key_hbm, value_hbm, query_hbm)):
        copy = pltpu.make_async_remote_copy(
            src_ref=source.at[pl.ds(tokens - TAIL, TAIL)],
            dst_ref=tails.at[at],
            send_sem=tail_send.at[at],
            recv_sem=tail_recv.at[at],
            device_id=(after, ch),
            device_id_type=MESH,
        )
        copy.start()
        tail_copies.append(copy)
    for copy in cross_copies[:2]:
        copy.start()
    weight_copy.start()
    for copy in tail_copies:
        copy.wait_recv()
    for at in range(3):
        last = tails[at].astype(jnp.float32)[TAIL - BLOCK :]
        ext[at, 0:BLOCK] = jnp.where(me == 0, 0.0, last)
        ext[at, BLOCK:] = raw[at].astype(jnp.float32)

    def short_rows(at, filter_at, start):
        window = ext[at, pl.ds(start, 2 * BLOCK + BLOCK)]
        total = short_ref[filter_at, 0:1, :] * window[BLOCK:]
        for j in range(1, short_ref.shape[1]):
            total = total + short_ref[filter_at, j : j + 1, :] * window[BLOCK - j : 3 * BLOCK - j]
        return total

    @pl.loop(0, tokens // (2 * BLOCK))
    def _(i):
        start = pl.multiple_of(i * (2 * BLOCK), 2 * BLOCK)
        driven[pl.ds(start, 2 * BLOCK)] = short_rows(0, 1, start) * short_rows(1, 2, start)

    for part in range(2):
        columns = slice(part * half, (part + 1) * half)

        def advance(b, state):
            local_states[b, part] = state
            rows = driven[pl.ds(pl.multiple_of(b * BLOCK, BLOCK), BLOCK), columns]
            state = state * powers[BLOCK, part]
            for j in range(BLOCK):
                state = state + powers[BLOCK - 1 - j, part] * rows[j : j + 1, :]
            return state

        own_total[part] = lax.fori_loop(0, blocks, advance, jnp.zeros((order, half), jnp.float32))

    pair_copy = pltpu.make_async_remote_copy(
        src_ref=own_total,
        dst_ref=pair_total,
        send_sem=pair_send,
        recv_sem=pair_recv,
        device_id=(sibling, ch),
        device_id_type=MESH,
    )
    pair_copy.start()

    @pl.loop(0, tokens // (2 * BLOCK))
    def _(i):
        start = pl.multiple_of(i * (2 * BLOCK), 2 * BLOCK)
        query_buf[pl.ds(start, 2 * BLOCK)] = short_rows(2, 0, start).astype(query_buf.dtype)

    spread(0)
    pair_copy.wait_recv()
    my_rates = jnp.where(core == 0, rate_ref[:, 0:half], rate_ref[:, half:])
    mine = own_total[core]
    theirs = pair_total[core]
    first = jnp.where(core == 0, mine, theirs)
    second = jnp.where(core == 0, theirs, mine)
    step_decay = jnp.exp(-(my_rates * float(tokens)))
    ring_in[z] = first * step_decay + second

    ring_copies = []
    for at, peer in enumerate(ring_peers):
        copy = pltpu.make_async_remote_copy(
            src_ref=ring_in.at[z],
            dst_ref=ring_in.at[z],
            send_sem=ring_send.at[at],
            recv_sem=ring_recv.at[at],
            device_id=(peer, ch),
            device_id_type=MESH,
        )
        copy.start()
        ring_copies.append(copy)
    output_tables()
    spread(1)
    spread(2)
    for copy in ring_copies:
        copy.wait_recv()
    chip_decay = jnp.exp(-(my_rates * float(tokens * nc)))
    total = jnp.zeros((order, half), jnp.float32)
    before_me = total
    for at in range(nz):
        before_me = jnp.where(at == z, total, before_me)
        total = total * chip_decay + ring_in[at]
    plane_in[core, plane] = total
    carry_half[...] = before_me

    half_copy = pltpu.make_async_remote_copy(
        src_ref=carry_half,
        dst_ref=carry_in,
        send_sem=half_send,
        recv_sem=half_recv,
        device_id=(sibling, ch),
        device_id_type=MESH,
    )
    half_copy.start()

    def plane_copy(step, to_core, part):
        return pltpu.make_async_remote_copy(
            src_ref=plane_in.at[part, plane],
            dst_ref=plane_in.at[part, plane],
            send_sem=plane_send.at[step - 1, to_core],
            recv_sem=plane_recv.at[step - 1, part],
            device_id=(plane_peers[step - 1] + to_core, ch),
            device_id_type=MESH,
        )

    for step in range(1, planes):

        @pl.when(plane + step < planes)
        def _():
            for to_core in range(nc):
                plane_copy(step, to_core, core).start()

    spread(3)
    spread(4)
    second_hop(0)
    spread(5)
    second_hop(1)
    half_copy.wait_recv()
    for step in range(1, planes):

        @pl.when(plane >= step)
        def _():
            for part in range(nc):
                plane_copy(step, 0, part).wait_recv()

    distance = (z * (tokens * nc)).astype(jnp.float32)
    entries = []
    for part in range(2):
        columns = slice(part * half, (part + 1) * half)
        row_decay = jnp.exp(-(rate_ref[:, columns] * float(tokens * nc * nz)))
        earlier = jnp.zeros((order, half), jnp.float32)
        for at in range(planes - 1):
            earlier = jnp.where(at < plane, earlier * row_decay + plane_in[part, at], earlier)
        carry = jnp.where(core == part, carry_half[...], carry_in[...])
        carry = carry + earlier * jnp.exp(-(rate_ref[:, columns] * distance))
        decay = jnp.exp(-(rate_ref[:, columns] * float(tokens)))
        entries.append(jnp.where(core == 0, carry, carry * decay + pair_total[part]))
    out_rows = tokens // 2
    steps = out_rows // (2 * BLOCK)

    def output_half(which):
        for part in range(2):
            columns = slice(part * half, (part + 1) * half)
            decay = jnp.exp(-(rate_ref[:, columns] * float(out_rows)))
            entry_states[part] = jnp.where(which == 0, entries[part], entries[part] * decay)

        @pl.loop(0, steps)
        def _(step):
            i = which * steps + step
            start = pl.multiple_of(i * (2 * BLOCK), 2 * BLOCK)
            for part in range(2):
                columns = slice(part * half, (part + 1) * half)
                outs = []
                for sub in range(2):
                    entry = entry_states[part]
                    entry_states[part] = entry * powers[BLOCK, part]
                    state = local_states[2 * i + sub, part] + entry
                    rows = driven[pl.ds(pl.multiple_of(start + sub * BLOCK, BLOCK), BLOCK), columns]
                    out = taps[0, part] * rows
                    for n in range(1, BLOCK):
                        out = out + taps[n, part] * pltpu.roll(rows, n, 0)
                    for r in range(order):
                        out = out + response[r, :, columns] * state[r : r + 1, :]
                    outs.append(out)
                out = jnp.concatenate(outs, axis=0)
                query = query_buf[pl.ds(start, 2 * BLOCK), columns].astype(jnp.float32)
                gated_ref[pl.ds(start, 2 * BLOCK), columns] = (query * out).astype(gated_ref.dtype)

    keep = pl.multiple_of(ch * out_rows, out_rows)
    give = pl.multiple_of(other * out_rows, out_rows)
    arriving = rows_in.at[1, pl.ds(0, out_rows)]
    rows_copies = []
    for at, (source, slot, place, target) in enumerate(
        (
            (gated_ref.at[pl.ds(give, out_rows)], 1, 0, (me, other)),
            (gated_ref.at[pl.ds(keep, out_rows)], 0, 1, (sibling, ch)),
            (arriving, 1, 1, (sibling, ch)),
        )
    ):
        rows_copies.append(
            pltpu.make_async_remote_copy(
                src_ref=source,
                dst_ref=rows_in.at[slot, pl.ds(place * out_rows, out_rows)],
                send_sem=rows_send.at[at],
                recv_sem=rows_recv.at[at],
                device_id=target,
                device_id_type=MESH,
            )
        )
    output_half(other)
    rows_copies[0].start()
    second_hop(2)
    output_half(ch)
    rows_copies[1].start()
    rows_in[0, 0:out_rows] = gated_ref[pl.ds(keep, out_rows)]
    weight_copy.wait()
    rows_copies[1].wait_recv()

    @pl.loop(0, COLOURS)
    def _(n):
        columns = pl.ds(pl.multiple_of(n * piece_columns, piece_columns), piece_columns)
        partial[n] = jnp.dot(rows_in[0], own_weight[:, columns], preferred_element_type=jnp.float32)

    rows_copies[0].wait_recv()
    rows_copies[2].start()
    for direction in DIRECTIONS:
        for at in range(len(CHUNKS)):
            if (direction, at) not in arrived:
                spread_copies[direction, at].wait_recv()
        second_copies[direction].wait_recv()
    cross_copies[-1].wait_recv()
    rows_copies[2].wait_recv()

    def result_copy(n):
        column = pl.multiple_of(first_column + n * piece_columns, piece_columns)
        return pltpu.make_async_remote_copy(
            src_ref=to_sibling.at[n],
            dst_ref=out_ref.at[:, pl.ds(column, piece_columns)],
            send_sem=result_send.at[n],
            recv_sem=result_recv.at[n],
            device_id=(sibling, ch),
            device_id_type=MESH,
        )

    @pl.loop(0, COLOURS)
    def _(n):
        column = pl.multiple_of(first_column + n * piece_columns, piece_columns)
        total = partial[n] + jnp.dot(
            rows_in[1], other_weight[n], preferred_element_type=jnp.float32
        )
        total = total.astype(out_ref.dtype)
        to_sibling[n] = total[out_rows:]
        result_copy(n).start()
        out_ref[:, pl.ds(column, piece_columns)] = total[:out_rows]

    @pl.loop(0, COLOURS)
    def _(n):
        result_copy(n).wait()

    for step in range(1, planes):

        @pl.when(plane + step < planes)
        def _():
            for to_core in range(nc):
                plane_copy(step, to_core, core).wait_send()

    for copy in tail_copies + ring_copies + [pair_copy, half_copy]:
        copy.wait_send()
    for copy in cross_copies + rows_copies:
        copy.wait_send()
    for copy in list(spread_copies.values()) + list(second_copies.values()):
        copy.wait_send()


def scan_call(query_input, key_input, value_input, short_kernel, residues, rates, out_weight):
    nx, ny, nz, nc = SEQ_FACTORS
    tokens, width = query_input.shape
    order = rates.shape[0]
    half = width // 2
    columns = out_weight.shape[1]
    out_rows = tokens // 2
    piece_columns = columns // nc // COLOURS
    f32 = jnp.float32
    bf16 = jnp.bfloat16
    dma = pltpu.SemaphoreType.DMA
    vmem = pl.BlockSpec(memory_space=pltpu.VMEM)
    anywhere = pl.BlockSpec(memory_space=pl.ANY)
    return pl.pallas_call(
        scan_kernel,
        out_shape=jax.ShapeDtypeStruct((out_rows, columns), bf16),
        in_specs=[anywhere] * 3 + [vmem] * 3 + [anywhere],
        out_specs=vmem,
        scratch_shapes=[
            pltpu.VMEM((width, columns // nc), bf16),
            pltpu.VMEM((COLOURS, width, piece_columns), bf16),
            pltpu.VMEM((tokens, width), bf16),
            pltpu.VMEM((2, tokens, width), bf16),
            pltpu.VMEM((COLOURS, tokens, piece_columns), f32),
            pltpu.VMEM((COLOURS, out_rows, piece_columns), bf16),
            pltpu.VMEM((3, tokens, width), jnp.bfloat16),
            pltpu.VMEM((3, tokens + BLOCK, width), f32),
            pltpu.VMEM((3, TAIL, width), jnp.bfloat16),
            pltpu.VMEM((tokens, width), jnp.bfloat16),
            pltpu.VMEM((tokens, width), f32),
            pltpu.VMEM((tokens // BLOCK, 2, order, half), f32),
            pltpu.VMEM((2, order, half), f32),
            pltpu.VMEM((2, order, half), f32),
            pltpu.VMEM((BLOCK + 1, 2, order, half), f32),
            pltpu.VMEM((order, BLOCK, width), f32),
            pltpu.VMEM((BLOCK, 2, BLOCK, half), f32),
            pltpu.VMEM((2, order, half), f32),
            pltpu.VMEM((2, order, half), f32),
            pltpu.VMEM((nz, order, half), f32),
            pltpu.VMEM((order, half), f32),
            pltpu.VMEM((nc, nx * ny, order, half), f32),
            pltpu.VMEM((order, half), f32),
            pltpu.VMEM((order, half), f32),
            dma((3,)),
            dma((3,)),
            dma((3,)),
            dma,
            dma,
            dma((nz - 1,)),
            dma((nz - 1,)),
            dma((nx * ny - 1, nc)),
            dma((nx * ny - 1, nc)),
            dma,
            dma,
            dma,
            dma((len(CHUNKS) + 1,)),
            dma((len(CHUNKS) + 1,)),
            dma((len(DIRECTIONS), len(CHUNKS))),
            dma((len(DIRECTIONS), len(CHUNKS))),
            dma((len(DIRECTIONS),)),
            dma((len(DIRECTIONS),)),
            dma((3,)),
            dma((3,)),
            dma((COLOURS,)),
            dma((COLOURS,)),
        ],
        compiler_params=pltpu.CompilerParams(collective_id=0, has_side_effects=True, vmem_limit_bytes=48 << 20),
        name="long_scan",
    )(query_input, key_input, value_input, short_kernel, residues, rates, out_weight)


def per_device(query_input, key_input, value_input, short_kernel, residues, rates, out_weight):
    mixed = scan_call(
        query_input, key_input, value_input, short_kernel, residues, rates, out_weight
    )
    return mixed.astype(jnp.float32)


def solution(mesh):
    assert math.prod(SEQ_FACTORS) == mesh.shape["seq"]
    return jax.shard_map(
        per_device,
        mesh=mesh,
        in_specs=(
            P("seq", "ch"),
            P("seq", "ch"),
            P("seq", "ch"),
            P(None, None, "ch"),
            P(None, "ch"),
            P(None, "ch"),
            P("ch", None),
        ),
        out_specs=P(("seq", "ch"), None),
        check_vma=False,
    )
```

```python
import functools
import math

import jax
import jax.numpy as jnp
from jax import lax
from jax.experimental import pallas as pl
from jax.experimental.pallas import tpu as pltpu
from jax.sharding import PartitionSpec as P

SEQ_FACTORS = (2, 4, 8, 2)
MESH = pl.DeviceIdType.MESH
BLOCK = 8
TAIL = 16
COLOURS = 8
CHUNKS = ((0, 96), (96, 80), (176, 96), (272, 80), (352, 80), (432, 80))
PARTS = ((0, 176), (176, 176), (352, 160))
DIRECTIONS = ("x", "y+", "y-", "z+", "z-")
SECOND = {
    "x": (-1, 2, "z+"),
    "y+": (-1, 1, "z+"),
    "y-": (1, 1, "z-"),
    "z+": (-2, 0, "y+"),
    "z-": (2, 0, "y-"),
}


def scan_kernel(
    query_hbm,
    key_hbm,
    value_hbm,
    short_ref,
    residue_ref,
    rate_ref,
    weight_hbm,
    out_ref,
    own_weight,
    other_weight,
    gated_ref,
    rows_in,
    partial,
    to_sibling,
    raw,
    ext,
    tails,
    query_buf,
    driven,
    local_states,
    entry_states,
    first_state,
    state_rows,
    powers,
    response,
    taps,
    own_total,
    pair_total,
    ring_in,
    ring_total,
    plane_in,
    carry_half,
    carry_in,
    load_sem,
    tail_send,
    tail_recv,
    pair_send,
    pair_recv,
    ring_send,
    ring_recv,
    plane_send,
    plane_recv,
    half_send,
    half_recv,
    weight_sem,
    cross_send,
    cross_recv,
    spread_send,
    spread_recv,
    second_send,
    second_recv,
    rows_send,
    rows_recv,
    result_send,
    result_recv,
):
    nx, ny, nz, nc = SEQ_FACTORS
    planes = nx * ny
    devices = planes * nz * nc
    tokens, width = query_buf.shape
    half = width // 2
    blocks = tokens // BLOCK
    me = lax.axis_index("seq")
    ch = lax.axis_index("ch")
    core = lax.rem(me, nc)
    chip = lax.div(me, nc)
    z = lax.rem(chip, nz)
    plane = lax.div(chip, nz)
    after = lax.rem(me + 1, devices)
    before = lax.rem(me + devices - 1, devices)
    sibling = chip * nc + (1 - core)

    loads = []
    for at, source in enumerate((key_hbm, value_hbm, query_hbm)):
        copy = pltpu.make_async_copy(source, raw.at[at], load_sem.at[at])
        copy.start()
        loads.append(copy)

    ring_peers = []
    for step in range(1, nz):
        ring_peers.append((plane * nz + lax.rem(z + step, nz)) * nc + core)
    plane_peers = []
    for step in range(1, planes):
        plane_peers.append((lax.rem(plane + step, planes) * nz + z) * nc)
    x_low = lax.div(plane, ny)
    y = lax.rem(plane, ny)
    other = 1 - ch

    def seq_at(x_at, y_at, z_at):
        return ((x_at * ny + y_at) * nz + z_at) * nc + core

    neighbours = {
        "x": seq_at(1 - x_low, y, z),
        "y+": seq_at(x_low, lax.rem(y + 1, ny), z),
        "y-": seq_at(x_low, lax.rem(y + ny - 1, ny), z),
        "z+": seq_at(x_low, y, lax.rem(z + 1, nz)),
        "z-": seq_at(x_low, y, lax.rem(z + nz - 1, nz)),
    }
    across = neighbours["x"]
    peers = [(peer, ch) for peer in [after, before, sibling] + ring_peers]
    peers += [(peer + at, ch) for peer in plane_peers for at in range(nc)]
    peers += [(across, other), (me, other)]
    barrier = pltpu.get_barrier_semaphore()
    for peer in peers:
        pl.semaphore_signal(barrier, inc=1, device_id=peer, device_id_type=MESH)

    depth, own_columns = own_weight.shape
    piece_columns = own_columns // COLOURS
    first_column = core * own_columns
    colour = lax.rem(4 * x_low + 2 * y + z, COLOURS)

    def shifted(by):
        return lax.rem(colour + by + COLOURS, COLOURS)

    weight_copy = pltpu.make_async_copy(
        weight_hbm.at[:, pl.ds(pl.multiple_of(first_column, own_columns), own_columns)],
        own_weight,
        weight_sem,
    )

    def cross_copy(at, piece, start, size):
        column = pl.multiple_of(first_column + piece * piece_columns, piece_columns)
        return pltpu.make_async_remote_copy(
            src_ref=weight_hbm.at[pl.ds(start, size), pl.ds(column, piece_columns)],
            dst_ref=other_weight.at[piece, pl.ds(start, size)],
            send_sem=cross_send.at[at],
            recv_sem=cross_recv.at[at],
            device_id=(across, other),
            device_id_type=MESH,
        )

    cross_copies = [
        cross_copy(at, shifted(4), start, size) for at, (start, size) in enumerate(CHUNKS)
    ]
    cross_copies.append(cross_copy(len(CHUNKS), shifted(1), *PARTS[2]))

    def passed_on(direction, piece, start, size, send_sem, recv_sem):
        return pltpu.make_async_remote_copy(
            src_ref=other_weight.at[piece, pl.ds(start, size)],
            dst_ref=other_weight.at[piece, pl.ds(start, size)],
            send_sem=send_sem,
            recv_sem=recv_sem,
            device_id=(neighbours[direction], ch),
            device_id_type=MESH,
        )

    spread_copies = {}
    second_copies = {}
    for to, direction in enumerate(DIRECTIONS):
        for at, (start, size) in enumerate(CHUNKS):
            spread_copies[direction, at] = passed_on(
                direction, colour, start, size, spread_send.at[to, at], spread_recv.at[to, at]
            )
        by, part, _ = SECOND[direction]
        second_copies[direction] = passed_on(
            direction, shifted(by), *PARTS[part], second_send.at[to], second_recv.at[to]
        )

    def spread(at):
        cross_copies[at].wait_recv()
        if at + 2 < len(cross_copies):
            cross_copies[at + 2].start()
        for direction in DIRECTIONS:
            spread_copies[direction, at].start()

    def second_hop(part):
        for direction in DIRECTIONS:
            by, its_part, came = SECOND[direction]
            if its_part == part:
                for at in (2 * part, 2 * part + 1):
                    if (came, at) not in arrived:
                        arrived.add((came, at))
                        spread_copies[came, at].wait_recv()
                second_copies[direction].start()

    arrived = set()

    for part in range(2):
        columns = slice(part * half, (part + 1) * half)
        decay = jnp.exp(-rate_ref[:, columns])
        power = jnp.ones_like(decay)
        for n in range(BLOCK + 1):
            powers[n, part] = power
            power = power * decay
    order = rate_ref.shape[0]

    def output_tables():
        for part in range(2):
            columns = slice(part * half, (part + 1) * half)
            scaled = residue_ref[:, columns] * jnp.sqrt(2.0 * rate_ref[:, columns])
            rows = lax.broadcasted_iota(jnp.int32, (BLOCK, half), 0)
            for n in range(BLOCK):
                tap = jnp.sum(scaled * powers[n, part], axis=0, keepdims=True)
                taps[n, part] = jnp.where(rows >= n, jnp.broadcast_to(tap, (BLOCK, half)), 0.0)
        ages = lax.broadcasted_iota(jnp.int32, (BLOCK, width), 0).astype(jnp.float32) + 1.0
        for r in range(order):
            rate_row = rate_ref[r : r + 1, :]
            scale_row = residue_ref[r : r + 1, :] * jnp.sqrt(2.0 * rate_row)
            response[r] = scale_row * jnp.exp(-(ages * rate_row))

    pl.semaphore_wait(barrier, len(peers))
    for copy in loads:
        copy.wait()
    tail_copies = []
    for at, source in enumerate((key_hbm, value_hbm, query_hbm)):
        copy = pltpu.make_async_remote_copy(
            src_ref=source.at[pl.ds(tokens - TAIL, TAIL)],
            dst_ref=tails.at[at],
            send_sem=tail_send.at[at],
            recv_sem=tail_recv.at[at],
            device_id=(after, ch),
            device_id_type=MESH,
        )
        copy.start()
        tail_copies.append(copy)
    for copy in cross_copies[:2]:
        copy.start()
    weight_copy.start()
    for at in range(3):
        ext[at, BLOCK:] = raw[at].astype(jnp.float32)

    def short_rows(at, filter_at, start):
        window = ext[at, pl.ds(start, 2 * BLOCK + BLOCK)]
        total = short_ref[filter_at, 0:1, :] * window[BLOCK:]
        for j in range(1, short_ref.shape[1]):
            total = total + short_ref[filter_at, j : j + 1, :] * window[BLOCK - j : 3 * BLOCK - j]
        return total

    def drive(i):
        start = pl.multiple_of(i * (2 * BLOCK), 2 * BLOCK)
        driven[pl.ds(start, 2 * BLOCK)] = short_rows(0, 1, start) * short_rows(1, 2, start)

    def scan_blocks(first, last, part):
        columns = slice(part * half, (part + 1) * half)

        def advance(b, state):
            local_states[b, part] = state
            rows = driven[pl.ds(pl.multiple_of(b * BLOCK, BLOCK), BLOCK), columns]
            state = state * powers[BLOCK, part]
            for j in range(BLOCK):
                state = state + powers[BLOCK - 1 - j, part] * rows[j : j + 1, :]
            return state

        return lax.fori_loop(first, last, advance, jnp.zeros((order, half), jnp.float32))

    pl.loop(1, tokens // (2 * BLOCK))(drive)
    later = [scan_blocks(2, blocks, part) for part in range(2)]
    for copy in tail_copies:
        copy.wait_recv()
    for at in range(3):
        last = tails[at].astype(jnp.float32)[TAIL - BLOCK :]
        ext[at, 0:BLOCK] = jnp.where(me == 0, 0.0, last)
    pl.loop(0, 1)(drive)
    for part in range(2):
        columns = slice(part * half, (part + 1) * half)
        state = scan_blocks(0, 2, part)
        first_state[part] = state
        decay = jnp.exp(-(rate_ref[:, columns] * float(tokens - 2 * BLOCK)))
        own_total[part] = later[part] + state * decay

    pair_copy = pltpu.make_async_remote_copy(
        src_ref=own_total,
        dst_ref=pair_total,
        send_sem=pair_send,
        recv_sem=pair_recv,
        device_id=(sibling, ch),
        device_id_type=MESH,
    )
    pair_copy.start()

    @pl.loop(0, tokens // (2 * BLOCK))
    def _(i):
        start = pl.multiple_of(i * (2 * BLOCK), 2 * BLOCK)
        query_buf[pl.ds(start, 2 * BLOCK)] = short_rows(2, 0, start).astype(query_buf.dtype)

    spread(0)
    pair_copy.wait_recv()
    my_rates = jnp.where(core == 0, rate_ref[:, 0:half], rate_ref[:, half:])
    mine = own_total[core]
    theirs = pair_total[core]
    first = jnp.where(core == 0, mine, theirs)
    second = jnp.where(core == 0, theirs, mine)
    step_decay = jnp.exp(-(my_rates * float(tokens)))
    ring_in[z] = first * step_decay + second

    ring_copies = []
    for at, peer in enumerate(ring_peers):
        copy = pltpu.make_async_remote_copy(
            src_ref=ring_in.at[z],
            dst_ref=ring_in.at[z],
            send_sem=ring_send.at[at],
            recv_sem=ring_recv.at[at],
            device_id=(peer, ch),
            device_id_type=MESH,
        )
        copy.start()
        ring_copies.append(copy)
    output_tables()
    spread(1)
    spread(2)
    for copy in ring_copies:
        copy.wait_recv()
    chip_decay = jnp.exp(-(my_rates * float(tokens * nc)))
    total = jnp.zeros((order, half), jnp.float32)
    before_me = total
    for at in range(nz):
        before_me = jnp.where(at == z, total, before_me)
        total = total * chip_decay + ring_in[at]
    plane_in[core, plane] = total
    carry_half[...] = before_me

    half_copy = pltpu.make_async_remote_copy(
        src_ref=carry_half,
        dst_ref=carry_in,
        send_sem=half_send,
        recv_sem=half_recv,
        device_id=(sibling, ch),
        device_id_type=MESH,
    )
    half_copy.start()

    def plane_copy(step, to_core, part):
        return pltpu.make_async_remote_copy(
            src_ref=plane_in.at[part, plane],
            dst_ref=plane_in.at[part, plane],
            send_sem=plane_send.at[step - 1, to_core],
            recv_sem=plane_recv.at[step - 1, part],
            device_id=(plane_peers[step - 1] + to_core, ch),
            device_id_type=MESH,
        )

    for step in range(1, planes):

        @pl.when(plane + step < planes)
        def _():
            for to_core in range(nc):
                plane_copy(step, to_core, core).start()

    spread(3)
    spread(4)
    second_hop(0)
    spread(5)
    second_hop(1)
    half_copy.wait_recv()
    for step in range(1, planes):

        @pl.when(plane >= step)
        def _():
            for part in range(nc):
                plane_copy(step, 0, part).wait_recv()

    distance = (z * (tokens * nc)).astype(jnp.float32)
    entries = []
    for part in range(2):
        columns = slice(part * half, (part + 1) * half)
        row_decay = jnp.exp(-(rate_ref[:, columns] * float(tokens * nc * nz)))
        earlier = jnp.zeros((order, half), jnp.float32)
        for at in range(planes - 1):
            earlier = jnp.where(at < plane, earlier * row_decay + plane_in[part, at], earlier)
        carry = jnp.where(core == part, carry_half[...], carry_in[...])
        carry = carry + earlier * jnp.exp(-(rate_ref[:, columns] * distance))
        decay = jnp.exp(-(rate_ref[:, columns] * float(tokens)))
        entries.append(jnp.where(core == 0, carry, carry * decay + pair_total[part]))
    out_rows = tokens // 2
    steps = out_rows // (2 * BLOCK)

    def output_half(which):
        for part in range(2):
            columns = slice(part * half, (part + 1) * half)
            decay = jnp.exp(-(rate_ref[:, columns] * float(out_rows)))
            shift = jnp.exp(-(rate_ref[:, columns] * float(out_rows - 2 * BLOCK)))
            entry_states[part] = jnp.where(
                which == 0, entries[part], entries[part] * decay + first_state[part] * shift
            )

        @pl.loop(0, steps)
        def _(step):
            i = which * steps + step
            start = pl.multiple_of(i * (2 * BLOCK), 2 * BLOCK)
            for part in range(2):
                columns = slice(part * half, (part + 1) * half)
                outs = []
                for sub in range(2):
                    entry = entry_states[part]
                    following = entry * powers[BLOCK, part]
                    if sub == 1:
                        following = following + jnp.where(i == 0, first_state[part], 0.0)
                    entry_states[part] = following
                    state = local_states[2 * i + sub, part] + entry
                    rows = driven[pl.ds(pl.multiple_of(start + sub * BLOCK, BLOCK), BLOCK), columns]
                    out = taps[0, part] * rows
                    for n in range(1, BLOCK):
                        out = out + taps[n, part] * pltpu.roll(rows, n, 0)
                    for r in range(order):
                        out = out + response[r, :, columns] * state[r : r + 1, :]
                    outs.append(out)
                out = jnp.concatenate(outs, axis=0)
                query = query_buf[pl.ds(start, 2 * BLOCK), columns].astype(jnp.float32)
                gated_ref[pl.ds(start, 2 * BLOCK), columns] = (query * out).astype(gated_ref.dtype)

    keep = pl.multiple_of(ch * out_rows, out_rows)
    give = pl.multiple_of(other * out_rows, out_rows)
    arriving = rows_in.at[1, pl.ds(0, out_rows)]
    rows_copies = []
    for at, (source, slot, place, target) in enumerate(
        (
            (gated_ref.at[pl.ds(give, out_rows)], 1, 0, (me, other)),
            (gated_ref.at[pl.ds(keep, out_rows)], 0, 1, (sibling, ch)),
            (arriving, 1, 1, (sibling, ch)),
        )
    ):
        rows_copies.append(
            pltpu.make_async_remote_copy(
                src_ref=source,
                dst_ref=rows_in.at[slot, pl.ds(place * out_rows, out_rows)],
                send_sem=rows_send.at[at],
                recv_sem=rows_recv.at[at],
                device_id=target,
                device_id_type=MESH,
            )
        )
    output_half(other)
    rows_copies[0].start()
    second_hop(2)
    output_half(ch)
    rows_copies[1].start()
    rows_in[0, 0:out_rows] = gated_ref[pl.ds(keep, out_rows)]
    weight_copy.wait()
    rows_copies[1].wait_recv()

    @pl.loop(0, COLOURS)
    def _(n):
        columns = pl.ds(pl.multiple_of(n * piece_columns, piece_columns), piece_columns)
        partial[n] = jnp.dot(rows_in[0], own_weight[:, columns], preferred_element_type=jnp.float32)

    rows_copies[0].wait_recv()
    rows_copies[2].start()
    for direction in DIRECTIONS:
        for at in range(len(CHUNKS)):
            if (direction, at) not in arrived:
                spread_copies[direction, at].wait_recv()
        second_copies[direction].wait_recv()
    cross_copies[-1].wait_recv()
    rows_copies[2].wait_recv()

    def result_copy(n):
        column = pl.multiple_of(first_column + n * piece_columns, piece_columns)
        return pltpu.make_async_remote_copy(
            src_ref=to_sibling.at[n],
            dst_ref=out_ref.at[:, pl.ds(column, piece_columns)],
            send_sem=result_send.at[n],
            recv_sem=result_recv.at[n],
            device_id=(sibling, ch),
            device_id_type=MESH,
        )

    @pl.loop(0, COLOURS)
    def _(n):
        column = pl.multiple_of(first_column + n * piece_columns, piece_columns)
        total = partial[n] + jnp.dot(
            rows_in[1], other_weight[n], preferred_element_type=jnp.float32
        )
        total = total.astype(out_ref.dtype)
        to_sibling[n] = total[out_rows:]
        result_copy(n).start()
        out_ref[:, pl.ds(column, piece_columns)] = total[:out_rows]

    @pl.loop(0, COLOURS)
    def _(n):
        result_copy(n).wait()

    for step in range(1, planes):

        @pl.when(plane + step < planes)
        def _():
            for to_core in range(nc):
                plane_copy(step, to_core, core).wait_send()

    for copy in tail_copies + ring_copies + [pair_copy, half_copy]:
        copy.wait_send()
    for copy in cross_copies + rows_copies:
        copy.wait_send()
    for copy in list(spread_copies.values()) + list(second_copies.values()):
        copy.wait_send()


def scan_call(query_input, key_input, value_input, short_kernel, residues, rates, out_weight):
    nx, ny, nz, nc = SEQ_FACTORS
    tokens, width = query_input.shape
    order = rates.shape[0]
    half = width // 2
    columns = out_weight.shape[1]
    out_rows = tokens // 2
    piece_columns = columns // nc // COLOURS
    f32 = jnp.float32
    bf16 = jnp.bfloat16
    dma = pltpu.SemaphoreType.DMA
    vmem = pl.BlockSpec(memory_space=pltpu.VMEM)
    anywhere = pl.BlockSpec(memory_space=pl.ANY)
    return pl.pallas_call(
        scan_kernel,
        out_shape=jax.ShapeDtypeStruct((out_rows, columns), bf16),
        in_specs=[anywhere] * 3 + [vmem] * 3 + [anywhere],
        out_specs=vmem,
        scratch_shapes=[
            pltpu.VMEM((width, columns // nc), bf16),
            pltpu.VMEM((COLOURS, width, piece_columns), bf16),
            pltpu.VMEM((tokens, width), bf16),
            pltpu.VMEM((2, tokens, width), bf16),
            pltpu.VMEM((COLOURS, tokens, piece_columns), f32),
            pltpu.VMEM((COLOURS, out_rows, piece_columns), bf16),
            pltpu.VMEM((3, tokens, width), jnp.bfloat16),
            pltpu.VMEM((3, tokens + BLOCK, width), f32),
            pltpu.VMEM((3, TAIL, width), jnp.bfloat16),
            pltpu.VMEM((tokens, width), jnp.bfloat16),
            pltpu.VMEM((tokens, width), f32),
            pltpu.VMEM((tokens // BLOCK, 2, order, half), f32),
            pltpu.VMEM((2, order, half), f32),
            pltpu.VMEM((2, order, half), f32),
            pltpu.VMEM((2, order, half), f32),
            pltpu.VMEM((BLOCK + 1, 2, order, half), f32),
            pltpu.VMEM((order, BLOCK, width), f32),
            pltpu.VMEM((BLOCK, 2, BLOCK, half), f32),
            pltpu.VMEM((2, order, half), f32),
            pltpu.VMEM((2, order, half), f32),
            pltpu.VMEM((nz, order, half), f32),
            pltpu.VMEM((order, half), f32),
            pltpu.VMEM((nc, nx * ny, order, half), f32),
            pltpu.VMEM((order, half), f32),
            pltpu.VMEM((order, half), f32),
            dma((3,)),
            dma((3,)),
            dma((3,)),
            dma,
            dma,
            dma((nz - 1,)),
            dma((nz - 1,)),
            dma((nx * ny - 1, nc)),
            dma((nx * ny - 1, nc)),
            dma,
            dma,
            dma,
            dma((len(CHUNKS) + 1,)),
            dma((len(CHUNKS) + 1,)),
            dma((len(DIRECTIONS), len(CHUNKS))),
            dma((len(DIRECTIONS), len(CHUNKS))),
            dma((len(DIRECTIONS),)),
            dma((len(DIRECTIONS),)),
            dma((3,)),
            dma((3,)),
            dma((COLOURS,)),
            dma((COLOURS,)),
        ],
        compiler_params=pltpu.CompilerParams(collective_id=0, has_side_effects=True, vmem_limit_bytes=48 << 20),
        name="long_scan",
    )(query_input, key_input, value_input, short_kernel, residues, rates, out_weight)


def per_device(query_input, key_input, value_input, short_kernel, residues, rates, out_weight):
    arguments = (query_input, key_input, value_input, short_kernel, residues, rates, out_weight)
    mixed = scan_call(*[pltpu.with_memory_space_constraint(a, pltpu.HBM) for a in arguments])
    return mixed.astype(jnp.float32)


def solution(mesh):
    assert math.prod(SEQ_FACTORS) == mesh.shape["seq"]
    return jax.shard_map(
        per_device,
        mesh=mesh,
        in_specs=(
            P("seq", "ch"),
            P("seq", "ch"),
            P("seq", "ch"),
            P(None, None, "ch"),
            P(None, "ch"),
            P(None, "ch"),
            P("ch", None),
        ),
        out_specs=P(("seq", "ch"), None),
        check_vma=False,
    )
```

```python
import functools
import math

import jax
import jax.numpy as jnp
from jax import lax
from jax.experimental import pallas as pl
from jax.experimental.pallas import tpu as pltpu
from jax.sharding import PartitionSpec as P

SEQ_FACTORS = (2, 4, 8, 2)
MESH = pl.DeviceIdType.MESH
BLOCK = 8
TAIL = 16
COLOURS = 8
CHUNKS = ((0, 96), (96, 80), (176, 96), (272, 80), (352, 80), (432, 80))
PARTS = ((0, 176), (176, 176), (352, 160))
DIRECTIONS = ("x", "y+", "y-", "z+", "z-")
SECOND = {
    "x": (-1, 2, "z+"),
    "y+": (-1, 1, "z+"),
    "y-": (1, 1, "z-"),
    "z+": (-2, 0, "y+"),
    "z-": (2, 0, "y-"),
}


def scan_kernel(
    query_hbm,
    key_hbm,
    value_hbm,
    short_ref,
    residue_ref,
    rate_ref,
    weight_hbm,
    out_ref,
    own_weight,
    other_weight,
    gated_ref,
    rows_in,
    partial,
    to_sibling,
    raw,
    ext,
    tails,
    query_buf,
    driven,
    local_states,
    entry_states,
    first_state,
    state_rows,
    powers,
    response,
    taps,
    own_total,
    pair_total,
    ring_in,
    ring_total,
    plane_in,
    carry_half,
    carry_in,
    load_sem,
    tail_send,
    tail_recv,
    pair_send,
    pair_recv,
    ring_send,
    ring_recv,
    plane_send,
    plane_recv,
    half_send,
    half_recv,
    weight_sem,
    cross_send,
    cross_recv,
    spread_send,
    spread_recv,
    second_send,
    second_recv,
    rows_send,
    rows_recv,
    result_send,
    result_recv,
):
    nx, ny, nz, nc = SEQ_FACTORS
    planes = nx * ny
    devices = planes * nz * nc
    tokens, width = query_buf.shape
    half = width // 2
    blocks = tokens // BLOCK
    me = lax.axis_index("seq")
    ch = lax.axis_index("ch")
    core = lax.rem(me, nc)
    chip = lax.div(me, nc)
    z = lax.rem(chip, nz)
    plane = lax.div(chip, nz)
    after = lax.rem(me + 1, devices)
    before = lax.rem(me + devices - 1, devices)
    sibling = chip * nc + (1 - core)

    loads = []
    for at, source in enumerate((key_hbm, value_hbm, query_hbm)):
        copy = pltpu.make_async_copy(source, raw.at[at], load_sem.at[at])
        copy.start()
        loads.append(copy)

    ring_peers = []
    for step in range(1, nz):
        ring_peers.append((plane * nz + lax.rem(z + step, nz)) * nc + core)
    plane_peers = []
    for step in range(1, planes):
        plane_peers.append((lax.rem(plane + step, planes) * nz + z) * nc)
    x_low = lax.div(plane, ny)
    y = lax.rem(plane, ny)
    other = 1 - ch

    def seq_at(x_at, y_at, z_at):
        return ((x_at * ny + y_at) * nz + z_at) * nc + core

    neighbours = {
        "x": seq_at(1 - x_low, y, z),
        "y+": seq_at(x_low, lax.rem(y + 1, ny), z),
        "y-": seq_at(x_low, lax.rem(y + ny - 1, ny), z),
        "z+": seq_at(x_low, y, lax.rem(z + 1, nz)),
        "z-": seq_at(x_low, y, lax.rem(z + nz - 1, nz)),
    }
    across = neighbours["x"]
    peers = [(peer, ch) for peer in [after, before, sibling] + ring_peers]
    peers += [(peer + at, ch) for peer in plane_peers for at in range(nc)]
    peers += [(across, other), (me, other)]
    barrier = pltpu.get_barrier_semaphore()
    for peer in peers:
        pl.semaphore_signal(barrier, inc=1, device_id=peer, device_id_type=MESH)

    depth, own_columns = own_weight.shape
    piece_columns = own_columns // COLOURS
    first_column = core * own_columns
    colour = lax.rem(4 * x_low + 2 * y + z, COLOURS)

    def shifted(by):
        return lax.rem(colour + by + COLOURS, COLOURS)

    weight_copy = pltpu.make_async_copy(
        weight_hbm.at[:, pl.ds(pl.multiple_of(first_column, own_columns), own_columns)],
        own_weight,
        weight_sem,
    )

    def cross_copy(at, piece, start, size):
        column = pl.multiple_of(first_column + piece * piece_columns, piece_columns)
        return pltpu.make_async_remote_copy(
            src_ref=weight_hbm.at[pl.ds(start, size), pl.ds(column, piece_columns)],
            dst_ref=other_weight.at[piece, pl.ds(start, size)],
            send_sem=cross_send.at[at],
            recv_sem=cross_recv.at[at],
            device_id=(across, other),
            device_id_type=MESH,
        )

    cross_copies = [
        cross_copy(at, shifted(4), start, size) for at, (start, size) in enumerate(CHUNKS)
    ]
    cross_copies.append(cross_copy(len(CHUNKS), shifted(1), *PARTS[2]))

    def passed_on(direction, piece, start, size, send_sem, recv_sem):
        return pltpu.make_async_remote_copy(
            src_ref=other_weight.at[piece, pl.ds(start, size)],
            dst_ref=other_weight.at[piece, pl.ds(start, size)],
            send_sem=send_sem,
            recv_sem=recv_sem,
            device_id=(neighbours[direction], ch),
            device_id_type=MESH,
        )

    spread_copies = {}
    second_copies = {}
    for to, direction in enumerate(DIRECTIONS):
        for at, (start, size) in enumerate(CHUNKS):
            spread_copies[direction, at] = passed_on(
                direction, colour, start, size, spread_send.at[to, at], spread_recv.at[to, at]
            )
        by, part, _ = SECOND[direction]
        second_copies[direction] = passed_on(
            direction, shifted(by), *PARTS[part], second_send.at[to], second_recv.at[to]
        )

    def spread(at):
        cross_copies[at].wait_recv()
        if at + 2 < len(cross_copies):
            cross_copies[at + 2].start()
        for direction in DIRECTIONS:
            spread_copies[direction, at].start()

    def second_hop(part):
        for direction in DIRECTIONS:
            by, its_part, came = SECOND[direction]
            if its_part == part:
                for at in (2 * part, 2 * part + 1):
                    if (came, at) not in arrived:
                        arrived.add((came, at))
                        spread_copies[came, at].wait_recv()
                second_copies[direction].start()

    arrived = set()

    for part in range(2):
        columns = slice(part * half, (part + 1) * half)
        decay = jnp.exp(-rate_ref[:, columns])
        power = jnp.ones_like(decay)
        for n in range(BLOCK + 1):
            powers[n, part] = power
            power = power * decay
    order = rate_ref.shape[0]

    def output_tables():
        for part in range(2):
            columns = slice(part * half, (part + 1) * half)
            scaled = residue_ref[:, columns] * jnp.sqrt(2.0 * rate_ref[:, columns])
            rows = lax.broadcasted_iota(jnp.int32, (BLOCK, half), 0)
            for n in range(BLOCK):
                tap = jnp.sum(scaled * powers[n, part], axis=0, keepdims=True)
                taps[n, part] = jnp.where(rows >= n, jnp.broadcast_to(tap, (BLOCK, half)), 0.0)
        ages = lax.broadcasted_iota(jnp.int32, (BLOCK, width), 0).astype(jnp.float32) + 1.0
        for r in range(order):
            rate_row = rate_ref[r : r + 1, :]
            scale_row = residue_ref[r : r + 1, :] * jnp.sqrt(2.0 * rate_row)
            response[r] = scale_row * jnp.exp(-(ages * rate_row))

    pl.semaphore_wait(barrier, len(peers))
    tail_copies = []
    for at, source in enumerate((key_hbm, value_hbm, query_hbm)):
        copy = pltpu.make_async_remote_copy(
            src_ref=source.at[pl.ds(tokens - TAIL, TAIL)],
            dst_ref=tails.at[at],
            send_sem=tail_send.at[at],
            recv_sem=tail_recv.at[at],
            device_id=(after, ch),
            device_id_type=MESH,
        )
        copy.start()
        tail_copies.append(copy)
    for copy in cross_copies[:2]:
        copy.start()
    weight_copy.start()
    for copy in loads:
        copy.wait()
    for at in range(3):
        ext[at, BLOCK:] = raw[at].astype(jnp.float32)

    def short_rows(at, filter_at, start):
        window = ext[at, pl.ds(start, 2 * BLOCK + BLOCK)]
        total = short_ref[filter_at, 0:1, :] * window[BLOCK:]
        for j in range(1, short_ref.shape[1]):
            total = total + short_ref[filter_at, j : j + 1, :] * window[BLOCK - j : 3 * BLOCK - j]
        return total

    def drive(i):
        start = pl.multiple_of(i * (2 * BLOCK), 2 * BLOCK)
        driven[pl.ds(start, 2 * BLOCK)] = short_rows(0, 1, start) * short_rows(1, 2, start)

    def scan_blocks(first, last, part):
        columns = slice(part * half, (part + 1) * half)

        def advance(b, state):
            local_states[b, part] = state
            rows = driven[pl.ds(pl.multiple_of(b * BLOCK, BLOCK), BLOCK), columns]
            state = state * powers[BLOCK, part]
            for j in range(BLOCK):
                state = state + powers[BLOCK - 1 - j, part] * rows[j : j + 1, :]
            return state

        return lax.fori_loop(first, last, advance, jnp.zeros((order, half), jnp.float32))

    pl.loop(1, tokens // (2 * BLOCK))(drive)
    later = [scan_blocks(2, blocks, part) for part in range(2)]
    for copy in tail_copies:
        copy.wait_recv()
    for at in range(3):
        last = tails[at].astype(jnp.float32)[TAIL - BLOCK :]
        ext[at, 0:BLOCK] = jnp.where(me == 0, 0.0, last)
    pl.loop(0, 1)(drive)
    for part in range(2):
        columns = slice(part * half, (part + 1) * half)
        state = scan_blocks(0, 2, part)
        first_state[part] = state
        decay = jnp.exp(-(rate_ref[:, columns] * float(tokens - 2 * BLOCK)))
        own_total[part] = later[part] + state * decay

    pair_copy = pltpu.make_async_remote_copy(
        src_ref=own_total,
        dst_ref=pair_total,
        send_sem=pair_send,
        recv_sem=pair_recv,
        device_id=(sibling, ch),
        device_id_type=MESH,
    )
    pair_copy.start()

    @pl.loop(0, tokens // (2 * BLOCK))
    def _(i):
        start = pl.multiple_of(i * (2 * BLOCK), 2 * BLOCK)
        query_buf[pl.ds(start, 2 * BLOCK)] = short_rows(2, 0, start).astype(query_buf.dtype)

    spread(0)
    pair_copy.wait_recv()
    my_rates = jnp.where(core == 0, rate_ref[:, 0:half], rate_ref[:, half:])
    mine = own_total[core]
    theirs = pair_total[core]
    first = jnp.where(core == 0, mine, theirs)
    second = jnp.where(core == 0, theirs, mine)
    step_decay = jnp.exp(-(my_rates * float(tokens)))
    ring_in[z] = first * step_decay + second

    ring_copies = []
    for at, peer in enumerate(ring_peers):
        copy = pltpu.make_async_remote_copy(
            src_ref=ring_in.at[z],
            dst_ref=ring_in.at[z],
            send_sem=ring_send.at[at],
            recv_sem=ring_recv.at[at],
            device_id=(peer, ch),
            device_id_type=MESH,
        )
        copy.start()
        ring_copies.append(copy)
    output_tables()
    spread(1)
    spread(2)
    for copy in ring_copies:
        copy.wait_recv()
    chip_decay = jnp.exp(-(my_rates * float(tokens * nc)))
    total = jnp.zeros((order, half), jnp.float32)
    before_me = total
    for at in range(nz):
        before_me = jnp.where(at == z, total, before_me)
        total = total * chip_decay + ring_in[at]
    plane_in[core, plane] = total
    carry_half[...] = before_me

    half_copy = pltpu.make_async_remote_copy(
        src_ref=carry_half,
        dst_ref=carry_in,
        send_sem=half_send,
        recv_sem=half_recv,
        device_id=(sibling, ch),
        device_id_type=MESH,
    )
    half_copy.start()

    def plane_copy(step, to_core, part):
        return pltpu.make_async_remote_copy(
            src_ref=plane_in.at[part, plane],
            dst_ref=plane_in.at[part, plane],
            send_sem=plane_send.at[step - 1, to_core],
            recv_sem=plane_recv.at[step - 1, part],
            device_id=(plane_peers[step - 1] + to_core, ch),
            device_id_type=MESH,
        )

    for step in range(1, planes):

        @pl.when(plane + step < planes)
        def _():
            for to_core in range(nc):
                plane_copy(step, to_core, core).start()

    spread(3)
    spread(4)
    second_hop(0)
    spread(5)
    second_hop(1)
    half_copy.wait_recv()
    for step in range(1, planes):

        @pl.when(plane >= step)
        def _():
            for part in range(nc):
                plane_copy(step, 0, part).wait_recv()

    distance = (z * (tokens * nc)).astype(jnp.float32)
    entries = []
    for part in range(2):
        columns = slice(part * half, (part + 1) * half)
        row_decay = jnp.exp(-(rate_ref[:, columns] * float(tokens * nc * nz)))
        earlier = jnp.zeros((order, half), jnp.float32)
        for at in range(planes - 1):
            earlier = jnp.where(at < plane, earlier * row_decay + plane_in[part, at], earlier)
        carry = jnp.where(core == part, carry_half[...], carry_in[...])
        carry = carry + earlier * jnp.exp(-(rate_ref[:, columns] * distance))
        decay = jnp.exp(-(rate_ref[:, columns] * float(tokens)))
        entries.append(jnp.where(core == 0, carry, carry * decay + pair_total[part]))
    out_rows = tokens // 2
    steps = out_rows // (2 * BLOCK)

    def output_half(which):
        for part in range(2):
            columns = slice(part * half, (part + 1) * half)
            decay = jnp.exp(-(rate_ref[:, columns] * float(out_rows)))
            shift = jnp.exp(-(rate_ref[:, columns] * float(out_rows - 2 * BLOCK)))
            entry_states[part] = jnp.where(
                which == 0, entries[part], entries[part] * decay + first_state[part] * shift
            )

        @pl.loop(0, steps)
        def _(step):
            i = which * steps + step
            start = pl.multiple_of(i * (2 * BLOCK), 2 * BLOCK)
            for part in range(2):
                columns = slice(part * half, (part + 1) * half)
                outs = []
                for sub in range(2):
                    entry = entry_states[part]
                    following = entry * powers[BLOCK, part]
                    if sub == 1:
                        following = following + jnp.where(i == 0, first_state[part], 0.0)
                    entry_states[part] = following
                    state = local_states[2 * i + sub, part] + entry
                    rows = driven[pl.ds(pl.multiple_of(start + sub * BLOCK, BLOCK), BLOCK), columns]
                    out = taps[0, part] * rows
                    for n in range(1, BLOCK):
                        out = out + taps[n, part] * pltpu.roll(rows, n, 0)
                    for r in range(order):
                        out = out + response[r, :, columns] * state[r : r + 1, :]
                    outs.append(out)
                out = jnp.concatenate(outs, axis=0)
                query = query_buf[pl.ds(start, 2 * BLOCK), columns].astype(jnp.float32)
                gated_ref[pl.ds(start, 2 * BLOCK), columns] = (query * out).astype(gated_ref.dtype)

    keep = pl.multiple_of(ch * out_rows, out_rows)
    give = pl.multiple_of(other * out_rows, out_rows)
    arriving = rows_in.at[1, pl.ds(0, out_rows)]
    rows_copies = []
    for at, (source, slot, place, target) in enumerate(
        (
            (gated_ref.at[pl.ds(give, out_rows)], 1, 0, (me, other)),
            (gated_ref.at[pl.ds(keep, out_rows)], 0, 1, (sibling, ch)),
            (arriving, 1, 1, (sibling, ch)),
        )
    ):
        rows_copies.append(
            pltpu.make_async_remote_copy(
                src_ref=source,
                dst_ref=rows_in.at[slot, pl.ds(place * out_rows, out_rows)],
                send_sem=rows_send.at[at],
                recv_sem=rows_recv.at[at],
                device_id=target,
                device_id_type=MESH,
            )
        )
    output_half(other)
    rows_copies[0].start()
    second_hop(2)
    output_half(ch)
    rows_copies[1].start()
    rows_in[0, 0:out_rows] = gated_ref[pl.ds(keep, out_rows)]
    weight_copy.wait()
    rows_copies[1].wait_recv()

    @pl.loop(0, COLOURS)
    def _(n):
        columns = pl.ds(pl.multiple_of(n * piece_columns, piece_columns), piece_columns)
        partial[n] = jnp.dot(rows_in[0], own_weight[:, columns], preferred_element_type=jnp.float32)

    rows_copies[0].wait_recv()
    rows_copies[2].start()
    for direction in DIRECTIONS:
        for at in range(len(CHUNKS)):
            if (direction, at) not in arrived:
                spread_copies[direction, at].wait_recv()
    rows_copies[2].wait_recv()

    def result_copy(n):
        column = pl.multiple_of(first_column + n * piece_columns, piece_columns)
        return pltpu.make_async_remote_copy(
            src_ref=to_sibling.at[n],
            dst_ref=out_ref.at[:, pl.ds(column, piece_columns)],
            send_sem=result_send.at[n],
            recv_sem=result_recv.at[n],
            device_id=(sibling, ch),
            device_id_type=MESH,
        )

    def finish(n):
        column = pl.multiple_of(first_column + n * piece_columns, piece_columns)
        total = partial[n] + jnp.dot(
            rows_in[1], other_weight[n], preferred_element_type=jnp.float32
        )
        total = total.astype(out_ref.dtype)
        to_sibling[n] = total[out_rows:]
        result_copy(n).start()
        out_ref[:, pl.ds(column, piece_columns)] = total[:out_rows]

    @pl.loop(0, COLOURS - 2)
    def _(k):
        finish(shifted(k + (k >= 3).astype(jnp.int32) + (k >= 4).astype(jnp.int32)))

    for direction in DIRECTIONS:
        second_copies[direction].wait_recv()
    cross_copies[-1].wait_recv()

    @pl.loop(0, 2)
    def _(k):
        finish(shifted(3 + 2 * k))

    @pl.loop(0, COLOURS)
    def _(n):
        result_copy(n).wait()

    for step in range(1, planes):

        @pl.when(plane + step < planes)
        def _():
            for to_core in range(nc):
                plane_copy(step, to_core, core).wait_send()

    for copy in tail_copies + ring_copies + [pair_copy, half_copy]:
        copy.wait_send()
    for copy in cross_copies + rows_copies:
        copy.wait_send()
    for copy in list(spread_copies.values()) + list(second_copies.values()):
        copy.wait_send()


def scan_call(query_input, key_input, value_input, short_kernel, residues, rates, out_weight):
    nx, ny, nz, nc = SEQ_FACTORS
    tokens, width = query_input.shape
    order = rates.shape[0]
    half = width // 2
    columns = out_weight.shape[1]
    out_rows = tokens // 2
    piece_columns = columns // nc // COLOURS
    f32 = jnp.float32
    bf16 = jnp.bfloat16
    dma = pltpu.SemaphoreType.DMA
    vmem = pl.BlockSpec(memory_space=pltpu.VMEM)
    anywhere = pl.BlockSpec(memory_space=pl.ANY)
    return pl.pallas_call(
        scan_kernel,
        out_shape=jax.ShapeDtypeStruct((out_rows, columns), bf16),
        in_specs=[anywhere] * 3 + [vmem] * 3 + [anywhere],
        out_specs=vmem,
        scratch_shapes=[
            pltpu.VMEM((width, columns // nc), bf16),
            pltpu.VMEM((COLOURS, width, piece_columns), bf16),
            pltpu.VMEM((tokens, width), bf16),
            pltpu.VMEM((2, tokens, width), bf16),
            pltpu.VMEM((COLOURS, tokens, piece_columns), f32),
            pltpu.VMEM((COLOURS, out_rows, piece_columns), bf16),
            pltpu.VMEM((3, tokens, width), jnp.bfloat16),
            pltpu.VMEM((3, tokens + BLOCK, width), f32),
            pltpu.VMEM((3, TAIL, width), jnp.bfloat16),
            pltpu.VMEM((tokens, width), jnp.bfloat16),
            pltpu.VMEM((tokens, width), f32),
            pltpu.VMEM((tokens // BLOCK, 2, order, half), f32),
            pltpu.VMEM((2, order, half), f32),
            pltpu.VMEM((2, order, half), f32),
            pltpu.VMEM((2, order, half), f32),
            pltpu.VMEM((BLOCK + 1, 2, order, half), f32),
            pltpu.VMEM((order, BLOCK, width), f32),
            pltpu.VMEM((BLOCK, 2, BLOCK, half), f32),
            pltpu.VMEM((2, order, half), f32),
            pltpu.VMEM((2, order, half), f32),
            pltpu.VMEM((nz, order, half), f32),
            pltpu.VMEM((order, half), f32),
            pltpu.VMEM((nc, nx * ny, order, half), f32),
            pltpu.VMEM((order, half), f32),
            pltpu.VMEM((order, half), f32),
            dma((3,)),
            dma((3,)),
            dma((3,)),
            dma,
            dma,
            dma((nz - 1,)),
            dma((nz - 1,)),
            dma((nx * ny - 1, nc)),
            dma((nx * ny - 1, nc)),
            dma,
            dma,
            dma,
            dma((len(CHUNKS) + 1,)),
            dma((len(CHUNKS) + 1,)),
            dma((len(DIRECTIONS), len(CHUNKS))),
            dma((len(DIRECTIONS), len(CHUNKS))),
            dma((len(DIRECTIONS),)),
            dma((len(DIRECTIONS),)),
            dma((3,)),
            dma((3,)),
            dma((COLOURS,)),
            dma((COLOURS,)),
        ],
        compiler_params=pltpu.CompilerParams(collective_id=0, has_side_effects=True, vmem_limit_bytes=48 << 20),
        name="long_scan",
    )(query_input, key_input, value_input, short_kernel, residues, rates, out_weight)


def per_device(query_input, key_input, value_input, short_kernel, residues, rates, out_weight):
    arguments = (query_input, key_input, value_input, short_kernel, residues, rates, out_weight)
    mixed = scan_call(*[pltpu.with_memory_space_constraint(a, pltpu.HBM) for a in arguments])
    return mixed.astype(jnp.float32)


def solution(mesh):
    assert math.prod(SEQ_FACTORS) == mesh.shape["seq"]
    return jax.shard_map(
        per_device,
        mesh=mesh,
        in_specs=(
            P("seq", "ch"),
            P("seq", "ch"),
            P("seq", "ch"),
            P(None, None, "ch"),
            P(None, "ch"),
            P(None, "ch"),
            P("ch", None),
        ),
        out_specs=P(("seq", "ch"), None),
        check_vma=False,
    )
```
